32 devices in a mesh: pipe: 4 (over y, x), ctx: 8 (over z, core).
Axes of the slice: x: 2, y: 2, z: 4, core: 2. Of those that a mesh axis runs over, the one named last changes fastest.
Arguments:
- ssm_input: bfloat16 [4, 3072, 4096], P('pipe', 'ctx'), may hold values from -0.078125 to 0.078125
- input_proj: bfloat16 [4, 3072, 512], P('pipe', 'ctx'), may hold values from -0.25 to 0.25
- output_proj: bfloat16 [4, 3072, 512], P('pipe', 'ctx'), may hold values from -0.25 to 0.25
- log_decay: float32 [4, 64, 3072], P('pipe', None, 'ctx'), may hold values from -2 to 0, as said below
- grad_output: bfloat16 [4, 3072, 4096], P('pipe', 'ctx'), may hold values from -6 to 6
- skip_gain: float32 [4, 64], P('pipe'), may hold values from 0.5 to 1.5
Outputs:
- grad_passed: bfloat16 [4, 3072, 4096], P('pipe', 'ctx')
- grad_input_proj: bfloat16 [4, 3072, 512], P('pipe', 'ctx')
- grad_output_proj: bfloat16 [4, 3072, 512], P('pipe', 'ctx')
- grad_decay: float32 [4, 64, 3072], P('pipe', None, 'ctx')
The draws below stay inside these ranges and needn't reach their ends.
Inputs may be any that keep to these rules, and one draw needn't show every extreme that they name: log_decay is never positive.
All inputs are finite; a program needn't handle non-finite values.
Results may differ from the reference program's by a relative error of at most 0.012.
Values may be sent and summed in bfloat16 or wider, within the bound.
A program may use at most 128 MiB of HBM per device.

```python
import jax
import jax.numpy as jnp
from jax import lax

TOK_DEV = 384
H = 64
P_SIZE = 64
N = 128
G = 4
HPG = 16
RELAY_LAYERS = 4
SEQUENCE_TOKENS = 3072
N_CTX = 8


def draw_log_decay(key, part):
    random_keys = jax.random.split(key, 7)
    blocks = SEQUENCE_TOKENS // TOK_DEV
    keep_share = 0.5
    slow_heads = jax.random.uniform(random_keys[0], (RELAY_LAYERS, H, 1)) < keep_share
    slow_rate = jnp.exp(jax.random.uniform(random_keys[1], (RELAY_LAYERS, H, 1), minval=jnp.log(0.1), maxval=jnp.log(0.4))) / SEQUENCE_TOKENS
    fast_rate = jnp.exp(jax.random.uniform(random_keys[2], (RELAY_LAYERS, H, 1), minval=jnp.log(1.0 / 25.0), maxval=jnp.log(1.0 / 12.0)))
    roughness = jnp.exp(jax.random.uniform(random_keys[3], (RELAY_LAYERS, H, blocks, TOK_DEV), minval=jnp.log(0.5), maxval=jnp.log(2.0)))
    device_factor = jnp.exp(jax.random.uniform(random_keys[4], (RELAY_LAYERS, H, blocks, 1), minval=jnp.log(0.5), maxval=jnp.log(2.0)))
    perturbed_input = (roughness * device_factor).reshape(RELAY_LAYERS, H, SEQUENCE_TOKENS)
    spike_positions = jax.random.randint(random_keys[5], (RELAY_LAYERS, 1, 1, 2), 0, SEQUENCE_TOKENS)
    spike_loss = jax.random.uniform(random_keys[6], (RELAY_LAYERS, 1, 1, 2), minval=0.2, maxval=0.5)
    token_positions = jnp.arange(SEQUENCE_TOKENS, dtype=jnp.int32)[None, None, :, None]
    spike_value = jnp.sum(jnp.where(token_positions == spike_positions, -jnp.log(1.0 - spike_loss), 0.0), axis=3)
    decay_rate = jnp.where(slow_heads, slow_rate, fast_rate)
    return (-(decay_rate * perturbed_input + spike_value)).astype(jnp.float32)


def shard_levels(rng, shape, shards, low, largest):
    factor_of, own = 1.0, jax.random.fold_in(rng, 6)
    for axis_at, shards_of in shards:
        draws = jnp.exp(jax.random.uniform(jax.random.fold_in(own, axis_at), (shards_of,), jnp.float32, low / len(shards), largest / len(shards)))
        factor_of = factor_of * jnp.repeat(draws, shape[axis_at] // shards_of).reshape([-1 if axis == axis_at else 1 for axis in range(len(shape))])
    return factor_of


def scatter_about(key, shape, spread, reach, shards=(), kind=jnp.bfloat16):
    level = shard_levels(key, shape, shards, -0.22, 0.18) if shards else 1.0
    array = jax.random.normal(key, shape, jnp.float32) * spread * level
    return jnp.minimum(jnp.maximum(array, -reach), reach).astype(kind)


def setup_inputs(seed: int = 0) -> dict:
    key_list = jax.random.split(jax.random.key(seed), 7)
    return {
        "ssm_input": scatter_about(key_list[0], (RELAY_LAYERS, SEQUENCE_TOKENS, H * P_SIZE), ((N * SEQUENCE_TOKENS) ** 0.25 / (P_SIZE * HPG * SEQUENCE_TOKENS) ** 0.5), 0.078125, ((0, 4), (1, 8))),
        "input_proj": scatter_about(key_list[1], (RELAY_LAYERS, SEQUENCE_TOKENS, G * N), (1 / (N * SEQUENCE_TOKENS) ** 0.25), 0.25, ((0, 4), (1, 8))),
        "output_proj": scatter_about(key_list[2], (RELAY_LAYERS, SEQUENCE_TOKENS, G * N), (1 / (N * SEQUENCE_TOKENS) ** 0.25), 0.25, ((0, 4), (1, 8))),
        "log_decay": draw_log_decay(jax.random.fold_in(key_list[6], 71), 0),
        "grad_output": scatter_about(key_list[4], (RELAY_LAYERS, SEQUENCE_TOKENS, H * P_SIZE), 1.0, 6.0, ((0, 4), (1, 8))),
        "skip_gain": jnp.clip(0.5 + 1.0 * jax.random.uniform(key_list[5], (RELAY_LAYERS, H), jnp.float32) ** shard_levels(key_list[5], (RELAY_LAYERS, H), ((0, 4),), -0.2, 0.2), 0.5, 1.5),
    }


far_below = -1.0e30
highest = lax.Precision.HIGHEST


def wide_einsum(formula, left, right):
    return jnp.einsum(formula, left.astype(jnp.float32), right.astype(jnp.float32), precision=highest)


def block_setup(ssm_block, input_block, output_block, decay_block, grad_block):
    length = ssm_block.shape[0]
    cumulative = jnp.cumsum(decay_block, axis=1)
    totals = cumulative[:, -1]
    end_weight = jnp.exp(totals[:, None] - cumulative)
    start_weight = jnp.exp(cumulative)
    inputs_heads = ssm_block.reshape(length, H, P_SIZE).astype(jnp.float32)
    grads_heads = grad_block.reshape(length, H, P_SIZE).astype(jnp.float32)
    input_weighted = (end_weight.T[:, :, None] * inputs_heads).astype(jnp.bfloat16)
    grad_weighted = (start_weight.T[:, :, None] * grads_heads).astype(jnp.bfloat16)
    input_groups = input_block.reshape(length, G, N)
    output_groups = output_block.reshape(length, G, N)
    state_local = wide_einsum("sgn,sgkp->gknp", input_groups, input_weighted.reshape(length, G, HPG, P_SIZE)).reshape(H, N, P_SIZE)
    adjoint_local = wide_einsum("tgn,tgkp->gknp", output_groups, grad_weighted.reshape(length, G, HPG, P_SIZE)).reshape(H, N, P_SIZE)
    return cumulative, totals, end_weight, start_weight, input_weighted, grad_weighted, state_local, adjoint_local


def group_grads(inputs_group, grads_group, input_group, output_group, cumulative, totals, end_weight, start_weight, input_weighted, grad_weighted, skip_part, entering, adjoint):
    length = inputs_group.shape[0]
    later = lax.broadcasted_iota(jnp.int32, (length, length), 0)
    earlier = lax.broadcasted_iota(jnp.int32, (length, length), 1)
    cum_gap = cumulative[:, :, None] - cumulative[:, None, :]
    kernel = jnp.exp(jnp.where((later >= earlier)[None], cum_gap, far_below))
    inner_prod = wide_einsum("tn,sn->ts", output_group, input_group)
    pair_prod = wide_einsum("tkp,skp->kts", grads_group, inputs_group)
    kernel_inner = kernel * inner_prod[None]
    joint_terms = kernel_inner * pair_prod
    cum_grad = jnp.sum(joint_terms, axis=2) - jnp.sum(joint_terms, axis=1)
    mixed_terms = jnp.sum(kernel * pair_prod, axis=0).astype(jnp.bfloat16)
    grad_local = wide_einsum("kts,tkp->skp", kernel_inner.astype(jnp.bfloat16), grads_group)
    input_local = wide_einsum("ts,tn->sn", mixed_terms, output_group)
    output_local = wide_einsum("ts,sn->tn", mixed_terms, input_group)
    entering_low = entering.astype(jnp.bfloat16)
    adjoint_low = adjoint.astype(jnp.bfloat16)
    grad_edge = end_weight.T[:, :, None] * wide_einsum("tn,knp->tkp", input_group, adjoint_low)
    right_edge = wide_einsum("tkp,knp->ktn", input_weighted, adjoint_low)
    left_edge = wide_einsum("tkp,knp->ktn", grad_weighted, entering_low)
    right_terms = jnp.sum(right_edge * input_group.astype(jnp.float32)[None], axis=2)
    left_terms = jnp.sum(left_edge * output_group.astype(jnp.float32)[None], axis=2)
    cross_term = jnp.exp(totals) * jnp.sum(entering * adjoint, axis=(1, 2))
    cum_grad = cum_grad + left_terms - right_terms
    cum_grad = cum_grad.at[:, -1].add(jnp.sum(right_terms, axis=1) + cross_term)
    grad_decay = jnp.cumsum(cum_grad[:, ::-1], axis=1)[:, ::-1]
    grad_x = (grad_local + grad_edge + skip_part[None, :, None] * grads_group.astype(jnp.float32)).astype(jnp.bfloat16)
    grad_b = (input_local + jnp.sum(right_edge, axis=0)).astype(jnp.bfloat16)
    grad_c = (output_local + jnp.sum(left_edge, axis=0)).astype(jnp.bfloat16)
    return grad_x.reshape(length, HPG * P_SIZE), grad_b, grad_c, grad_decay


def block_grads(ssm_block, input_block, output_block, decay_block, grad_block, skip_row, entering, adjoint):
    length = ssm_block.shape[0]
    cumulative, totals, end_weight, start_weight, input_weighted, grad_weighted, state_local, adjoint_local = block_setup(ssm_block, input_block, output_block, decay_block, grad_block)
    inputs_heads = ssm_block.reshape(length, H, P_SIZE)
    grads_heads = grad_block.reshape(length, H, P_SIZE)
    results = []
    for group_index in range(G):
        head_span = slice(group_index * HPG, (group_index + 1) * HPG)
        col_span = slice(group_index * N, (group_index + 1) * N)
        results.append(group_grads(inputs_heads[:, head_span], grads_heads[:, head_span], input_block[:, col_span], output_block[:, col_span], cumulative[head_span], totals[head_span], end_weight[head_span], start_weight[head_span], input_weighted[:, head_span], grad_weighted[:, head_span], skip_row[head_span], entering[head_span], adjoint[head_span]))
    grad_x = jnp.concatenate([item[0] for item in results], axis=1)
    grad_b = jnp.concatenate([item[1] for item in results], axis=1)
    grad_c = jnp.concatenate([item[2] for item in results], axis=1)
    grad_decay = jnp.concatenate([item[3] for item in results], axis=0)
    return grad_x, grad_b, grad_c, grad_decay


def carry_states(totals, pieces, reverse):
    def advance(state_acc, element):
        total_row, piece = element
        return jnp.exp(total_row)[:, None, None] * state_acc + piece, state_acc

    start_state = jnp.zeros(pieces.shape[1:], jnp.float32)
    _, entering = lax.scan(advance, start_state, (totals, pieces), reverse=reverse)
    return entering


def section_grads(ssm_section, input_section, output_section, decay_section, grad_section, skip_row):
    blocks = N_CTX
    ssm_blocks = ssm_section.reshape(blocks, TOK_DEV, H * P_SIZE)
    input_blocks = input_section.reshape(blocks, TOK_DEV, G * N)
    output_blocks = output_section.reshape(blocks, TOK_DEV, G * N)
    grad_blocks = grad_section.reshape(blocks, TOK_DEV, H * P_SIZE)
    decay_blocks = decay_section.reshape(H, blocks, TOK_DEV).transpose(1, 0, 2)

    def block_ends(element):
        setup = block_setup(*element)
        return setup[1], setup[6], setup[7]

    totals, state_local, adjoint_local = lax.map(block_ends, (ssm_blocks, input_blocks, output_blocks, decay_blocks, grad_blocks))
    entering = carry_states(totals, state_local, False)
    adjoint = carry_states(totals, adjoint_local, True)

    def block_work(element):
        return block_grads(element[0], element[1], element[2], element[3], element[4], skip_row, element[5], element[6])

    grad_x, grad_b, grad_c, grad_decay = lax.map(block_work, (ssm_blocks, input_blocks, output_blocks, decay_blocks, grad_blocks, entering, adjoint))
    return (grad_x.reshape(SEQUENCE_TOKENS, H * P_SIZE), grad_b.reshape(SEQUENCE_TOKENS, G * N), grad_c.reshape(SEQUENCE_TOKENS, G * N), grad_decay.transpose(1, 0, 2).reshape(H, SEQUENCE_TOKENS))


def reference(ssm_input, input_proj, output_proj, log_decay, grad_output, skip_gain):
    grads_x = []
    grads_b = []
    grads_c = []
    grads_d = []
    for section_index in range(RELAY_LAYERS):
        section_out = section_grads(ssm_input[section_index], input_proj[section_index], output_proj[section_index], log_decay[section_index], grad_output[section_index], skip_gain[section_index])
        grads_x.append(section_out[0])
        grads_b.append(section_out[1])
        grads_c.append(section_out[2])
        grads_d.append(section_out[3])
    grad_stack = jnp.stack(grads_x)
    grad_passed = jnp.concatenate([grad_stack[1:], grad_stack[:1]], axis=0)
    return grad_passed, jnp.stack(grads_b), jnp.stack(grads_c), jnp.stack(grads_d)
```

```python
import functools

import jax
import jax.numpy as jnp
from jax import lax
from jax.experimental import pallas as pl
from jax.experimental.pallas import tpu as pltpu
from jax.sharding import PartitionSpec as P

H = 64
P_SIZE = 64
N = 128
G = 4
HPG = 16
W = HPG * P_SIZE
Q = 128
PIECES = 8
LOG2E = 1.4426950408889634
MESH = pl.DeviceIdType.MESH
F32 = jnp.float32
BF16 = jnp.bfloat16


def dot(a, b, ca=1, cb=0):
    return lax.dot_general(a, b, (((ca,), (cb,)), ((), ())), preferred_element_type=F32)


def iota(shape, axis):
    return lax.broadcasted_iota(jnp.int32, shape, axis)


def split3(value):
    high = value.astype(BF16)
    rest = value - high.astype(F32)
    middle = rest.astype(BF16)
    return high, middle, (rest - middle.astype(F32)).astype(BF16)


def ones_where(condition):
    return jnp.where(condition, 1.0, 0.0).astype(BF16)


def spread_matrix():
    shape = (2 * HPG, W)
    return ones_where(iota(shape, 0) % HPG == iota(shape, 1) // P_SIZE)


def spread(weights, matrix):
    high = weights.astype(BF16)
    low = (weights - high.astype(F32)).astype(BF16)
    first = iota(weights.shape, 1) < HPG
    return dot(jnp.where(first, high.astype(F32), low.astype(F32)).astype(BF16), matrix)


def columns_cumulative(decay, lower):
    twice = jnp.concatenate([decay, decay], axis=0)
    return sum(dot(lower, part, 1, 1) for part in split3(twice))


def relay_kernel(n, per, s_ref, a_ref, e_ref, ent_ref, adj_ref, fs, bs, fsend, frecv, bsend, brecv):
    me = lax.axis_index("ctx")
    pipe = lax.axis_index("pipe")
    right, left = lax.rem(me + 1, n), lax.rem(me + n - 1, n)
    barrier = pltpu.get_barrier_semaphore()
    for neighbour in (left, right):
        pl.semaphore_signal(barrier, inc=1, device_id=(pipe, neighbour), device_id_type=MESH)
    pl.semaphore_wait(barrier, 2)

    def forward(k):
        return pltpu.make_async_remote_copy(
            src_ref=fs.at[k], dst_ref=ent_ref.at[k], send_sem=fsend.at[k], recv_sem=frecv.at[k],
            device_id=(pipe, right), device_id_type=MESH)

    def backward(k):
        return pltpu.make_async_remote_copy(
            src_ref=bs.at[k], dst_ref=adj_ref.at[k], send_sem=bsend.at[k], recv_sem=brecv.at[k],
            device_id=(pipe, left), device_id_type=MESH)

    def advance(k, place, make, got, local, sent):
        @pl.when(place > 0)
        def _():
            make(k).wait_recv()

        @pl.when(place == 0)
        def _():
            got[k] = jnp.zeros(got.shape[1:], BF16)

        @pl.when(place < n - 1)
        def _():
            sent[k] = (e_ref[k] * got[k].astype(F32) + local[k].astype(F32)).astype(BF16)
            make(k).start()

    def step(t, carry):
        kf = t - me
        kb = t - (n - 1 - me)

        @pl.when(jnp.logical_and(kf >= 0, kf < PIECES))
        def _():
            advance(kf, me, forward, ent_ref, s_ref, fs)

        @pl.when(jnp.logical_and(kb >= 0, kb < PIECES))
        def _():
            advance(kb, n - 1 - me, backward, adj_ref, a_ref, bs)

        return carry

    lax.fori_loop(0, n + PIECES - 1, step, 0)

    @pl.when(me < n - 1)
    def _():
        for k in range(PIECES):
            forward(k).wait_send()

    @pl.when(me > 0)
    def _():
        for k in range(PIECES):
            backward(k).wait_send()


def group_kernel(x_ref, b_ref, c_ref, decay_ref, g_ref, skip_ref, ent_ref, adj_ref,
                 gx_ref, db_ref, dc_ref, gd_ref,
                 xw_ref, gw_ref, end_ref, es_ref, ds_ref, edge_ref, cq_ref, cqt_ref, mixed_ref, row_ref, col_ref):
    chunks = x_ref.shape[0] // Q
    square = (Q, Q)
    lower = ones_where(iota(square, 1) <= iota(square, 0))
    upper = ones_where(iota(square, 0) <= iota(square, 1))
    matrix = spread_matrix()
    half = ent_ref.shape[2]

    for k in range(W // half):
        es_ref[0, :, k * half : (k + 1) * half] = ent_ref[k]
        ds_ref[chunks - 1, :, k * half : (k + 1) * half] = adj_ref[k]
    col_ref[...] = jnp.zeros(square, F32)
    keep = []
    for c in range(chunks):
        rows = slice(c * Q, (c + 1) * Q)
        decay = decay_ref[:, rows] * LOG2E
        cum = columns_cumulative(decay, lower)
        cqt_ref[c] = cum
        cq_ref[c] = sum(dot(part, upper) for part in split3(decay))
        end = spread(jnp.exp2(cum[Q - 1 : Q, :] - cum), matrix)
        start = spread(jnp.exp2(cum), matrix)
        end_ref[rows, :] = end
        xw_ref[rows, :] = (end * x_ref[rows, :].astype(F32)).astype(BF16)
        gw_ref[rows, :] = (start * g_ref[rows, :].astype(F32)).astype(BF16)
        keep.append(start[Q - 1 : Q, :])
    for c in range(chunks - 1):
        rows = slice(c * Q, (c + 1) * Q)
        local = dot(b_ref[rows, :], xw_ref[rows, :], 0, 0)
        es_ref[c + 1] = (keep[c] * es_ref[c].astype(F32) + local).astype(BF16)
    for c in range(chunks - 1, 0, -1):
        rows = slice(c * Q, (c + 1) * Q)
        local = dot(c_ref[rows, :], gw_ref[rows, :], 0, 0)
        ds_ref[c - 1] = (keep[c] * ds_ref[c].astype(F32) + local).astype(BF16)

    def chunk(c, carry):
        rows = pl.ds(pl.multiple_of(c * Q, Q), Q)
        bc = b_ref[rows, :]
        cc = c_ref[rows, :]
        valid = iota(square, 1) >= iota(square, 0)
        inner = jnp.where(valid, dot(bc, cc, 1, 1), 0.0)
        edge_ref[...] = dot(bc, ds_ref[c])
        cqt = cqt_ref[c]
        low_lane = iota(square, 1) < P_SIZE
        for pair in range(HPG // 2):
            lanes = slice(pair * 128, (pair + 1) * 128)
            xp = x_ref[rows, lanes]
            gp = g_ref[rows, lanes]
            zero = jnp.zeros_like(gp)
            gm = jnp.concatenate([jnp.where(low_lane, gp, zero), jnp.where(low_lane, zero, gp)], axis=0)
            pair_prod = dot(xp, gm, 1, 1)
            inners = []
            mixed = None
            for i in range(2):
                h = 2 * pair + i
                gap = jnp.minimum(cq_ref[c, h : h + 1, :] - cqt[:, h : h + 1], 0.0)
                kernel = jnp.exp2(gap)
                kp = kernel * pair_prod[:, i * Q : (i + 1) * Q]
                mixed = kp if mixed is None else mixed + kp
                inners.append((kernel * inner).astype(BF16))
                joint = kp * inner
                row_ref[h : h + 1, :] = jnp.sum(joint, axis=0, keepdims=True)
                col_ref[:, h : h + 1] = jnp.sum(joint, axis=1, keepdims=True)
            if pair == 0:
                mixed_ref[...] = mixed
            else:
                mixed_ref[...] += mixed
            local = dot(jnp.concatenate(inners, axis=1), gm)
            gx_ref[rows, lanes] = (
                local + end_ref[rows, lanes] * edge_ref[:, lanes] + skip_ref[:, lanes] * gp.astype(F32)
            ).astype(BF16)
        mixed_t = jnp.where(valid, mixed_ref[...], 0.0)
        xw = xw_ref[rows, :]
        gw = gw_ref[rows, :]
        ent = es_ref[c]
        adj = ds_ref[c]
        db_ref[rows, :] = (dot(mixed_t.astype(BF16), cc) + dot(xw, adj, 1, 1)).astype(BF16)
        dc_ref[rows, :] = (dot(mixed_t.T.astype(BF16), bc) + dot(gw, ent, 1, 1)).astype(BF16)
        right = xw.astype(F32) * edge_ref[...]
        left = gw.astype(F32) * dot(cc, ent)
        both = left - right
        high = both.astype(BF16)
        low = (both - high.astype(F32)).astype(BF16)
        heads = ones_where(iota((HPG, W), 0) == iota((HPG, W), 1) // P_SIZE)
        terms = dot(heads, high, 1, 1) + dot(heads, low, 1, 1)
        total = jnp.exp2(cq_ref[c][:, Q - 1 : Q])
        cross = jnp.sum(ent.astype(F32) * adj.astype(F32), axis=0, keepdims=True)
        rights = jnp.sum(right, axis=0, keepdims=True)
        wide = heads.astype(F32)
        last = total * jnp.sum(wide * cross, axis=1, keepdims=True) + jnp.sum(wide * rights, axis=1, keepdims=True)
        grads = row_ref[...] - col_ref[...].T[:HPG, :] + terms
        grads = grads + jnp.where(iota((HPG, Q), 1) == Q - 1, last, 0.0)
        gd_ref[c] = sum(dot(part, lower) for part in split3(grads))
        return carry

    lax.fori_loop(0, chunks, chunk, 0)


def local(ssm_input, input_proj, output_proj, log_decay, grad_output, skip_gain):
    x, b, c, decay, g = ssm_input[0], input_proj[0], output_proj[0], log_decay[0], grad_output[0]
    length = x.shape[0]
    chunks = length // Q
    n = lax.axis_size("ctx")
    half = G * W // PIECES
    skip = jnp.repeat(skip_gain, P_SIZE, axis=1)

    def in_specs(pick):
        return [
            pl.BlockSpec((length, W), lambda i: (0, pick(i))),
            pl.BlockSpec((length, N), lambda i: (0, pick(i))),
            pl.BlockSpec((length, N), lambda i: (0, pick(i))),
            pl.BlockSpec((HPG, length), lambda i: (pick(i), 0)),
            pl.BlockSpec((length, W), lambda i: (0, pick(i))),
        ]

    states = jax.ShapeDtypeStruct((PIECES, N, half), BF16)
    halves = W // half
    state_local, adjoint_local, kept = pl.pallas_call(
        functools.partial(setup_pieces, halves, half),
        grid=(G,),
        in_specs=in_specs(lambda i: i),
        out_specs=[
            pl.BlockSpec((halves, N, half), lambda i: (i, 0, 0)),
            pl.BlockSpec((halves, N, half), lambda i: (i, 0, 0)),
            pl.BlockSpec((halves, 1, half), lambda i: (i, 0, 0)),
        ],
        out_shape=[states, states, jax.ShapeDtypeStruct((PIECES, 1, half), F32)],
        compiler_params=pltpu.CompilerParams(vmem_limit_bytes=48 << 20),
        name="block_states",
    )(x, b, c, decay, g)

    whole = pl.BlockSpec(memory_space=pltpu.VMEM)
    entering, adjoint = pl.pallas_call(
        functools.partial(relay_kernel, n, half),
        in_specs=[whole] * 3,
        out_specs=[whole] * 2,
        out_shape=[states, states],
        scratch_shapes=[pltpu.VMEM((PIECES, N, half), BF16)] * 2 + [pltpu.SemaphoreType.DMA((PIECES,))] * 4,
        compiler_params=pltpu.CompilerParams(collective_id=0, has_side_effects=True, vmem_limit_bytes=32 << 20),
        name="relay",
    )(state_local, adjoint_local, kept)

    devices = lax.axis_size("pipe")
    route = [(source, (source - 1) % devices) for source in range(devices)]
    results = []
    for group in range(G):
        pick = functools.partial(lambda at, i: at, group)
        out = pl.pallas_call(
            group_kernel,
            grid=(1,),
            in_specs=in_specs(pick) + [
                pl.BlockSpec((1, W), lambda i, pick=pick: (0, pick(i))),
                pl.BlockSpec((halves, N, half), lambda i, pick=pick: (pick(i), 0, 0)),
                pl.BlockSpec((halves, N, half), lambda i, pick=pick: (pick(i), 0, 0)),
            ],
            out_specs=[
                pl.BlockSpec((length, W), lambda i: (0, 0)),
                pl.BlockSpec((length, N), lambda i: (0, 0)),
                pl.BlockSpec((length, N), lambda i: (0, 0)),
                pl.BlockSpec((chunks, HPG, Q), lambda i: (0, 0, 0)),
            ],
            out_shape=[
                jax.ShapeDtypeStruct((length, W), BF16),
                jax.ShapeDtypeStruct((length, N), BF16),
                jax.ShapeDtypeStruct((length, N), BF16),
                jax.ShapeDtypeStruct((chunks, HPG, Q), F32),
            ],
            scratch_shapes=[
                pltpu.VMEM((length, W), BF16),
                pltpu.VMEM((length, W), BF16),
                pltpu.VMEM((length, W), F32),
                pltpu.VMEM((chunks, N, W), BF16),
                pltpu.VMEM((chunks, N, W), BF16),
                pltpu.VMEM((Q, W), F32),
                pltpu.VMEM((chunks, HPG, Q), F32),
                pltpu.VMEM((chunks, Q, 2 * HPG), F32),
                pltpu.VMEM((Q, Q), F32),
                pltpu.VMEM((HPG, Q), F32),
                pltpu.VMEM((Q, Q), F32),
            ],
            compiler_params=pltpu.CompilerParams(vmem_limit_bytes=48 << 20),
            cost_estimate=pl.CostEstimate(flops=3_000_000_000, bytes_accessed=4_000_000, transcendentals=1_000_000),
            name="group_grads",
        )(x, b, c, decay, g, skip, entering, adjoint)
        results.append((lax.ppermute(out[0], "pipe", route),) + tuple(out[1:]))
    grad_x = jnp.concatenate([item[0] for item in results], axis=1)
    grad_b = jnp.concatenate([item[1] for item in results], axis=1)
    grad_c = jnp.concatenate([item[2] for item in results], axis=1)
    grad_decay = jnp.concatenate([item[3].transpose(1, 0, 2).reshape(HPG, length) for item in results], axis=0)
    return grad_x[None], grad_b[None], grad_c[None], grad_decay[None]


def setup_pieces(halves, half, x_ref, b_ref, c_ref, decay_ref, g_ref, s_ref, a_ref, e_ref):
    length = x_ref.shape[0]
    shape = (length, length)
    lower = ones_where(iota(shape, 1) <= iota(shape, 0))
    matrix = spread_matrix()
    cum = columns_cumulative(decay_ref[...] * LOG2E, lower)
    end = spread(jnp.exp2(cum[length - 1 : length, :] - cum), matrix)
    start = spread(jnp.exp2(cum), matrix)
    xw = (end * x_ref[...].astype(F32)).astype(BF16)
    gw = (start * g_ref[...].astype(F32)).astype(BF16)
    for k in range(halves):
        lanes = slice(k * half, (k + 1) * half)
        s_ref[k] = dot(b_ref[...], xw[:, lanes], 0, 0).astype(BF16)
        a_ref[k] = dot(c_ref[...], gw[:, lanes], 0, 0).astype(BF16)
        e_ref[k] = start[length - 1 : length, lanes]


def solution(mesh):
    return jax.shard_map(
        local,
        mesh=mesh,
        in_specs=(
            P("pipe", "ctx", None),
            P("pipe", "ctx", None),
            P("pipe", "ctx", None),
            P("pipe", None, "ctx"),
            P("pipe", "ctx", None),
            P("pipe", None),
        ),
        out_specs=(
            P("pipe", "ctx", None),
            P("pipe", "ctx", None),
            P("pipe", "ctx", None),
            P("pipe", None, "ctx"),
        ),
        check_vma=False,
    )
```

```python
import functools

import jax
import jax.numpy as jnp
from jax import lax
from jax.experimental import pallas as pl
from jax.experimental.pallas import tpu as pltpu
from jax.sharding import PartitionSpec as P

H = 64
P_SIZE = 64
N = 128
G = 4
HPG = 16
W = HPG * P_SIZE
Q = 128
PIECES = 8
RAW = 2
LOG2E = 1.4426950408889634
MESH = pl.DeviceIdType.MESH
F32 = jnp.float32
BF16 = jnp.bfloat16


def dot(a, b, ca=1, cb=0):
    return lax.dot_general(a, b, (((ca,), (cb,)), ((), ())), preferred_element_type=F32)


def iota(shape, axis):
    return lax.broadcasted_iota(jnp.int32, shape, axis)


def split3(value):
    high = value.astype(BF16)
    rest = value - high.astype(F32)
    middle = rest.astype(BF16)
    return high, middle, (rest - middle.astype(F32)).astype(BF16)


def ones_where(condition):
    return jnp.where(condition, 1.0, 0.0).astype(BF16)


def spread_matrix():
    shape = (2 * HPG, W)
    return ones_where(iota(shape, 0) % HPG == iota(shape, 1) // P_SIZE)


def spread(weights, matrix):
    high = weights.astype(BF16)
    low = (weights - high.astype(F32)).astype(BF16)
    first = iota(weights.shape, 1) < HPG
    return dot(jnp.where(first, high.astype(F32), low.astype(F32)).astype(BF16), matrix)


def columns_cumulative(decay, lower):
    twice = jnp.concatenate([decay, decay], axis=0)
    return sum(dot(lower, part, 1, 1) for part in split3(twice))


def relay_kernel(n, halves, half, x_hbm, b_hbm, c_hbm, decay_hbm, g_hbm, ent_ref, adj_ref,
                 xv, bv, cv, dv, gv, s_ref, a_ref, e_ref, fs, bs, small_sem, wide_sem, fsend, frecv, bsend, brecv):
    me = lax.axis_index("ctx")
    pipe = lax.axis_index("pipe")
    right, left = lax.rem(me + 1, n), lax.rem(me + n - 1, n)
    length = x_hbm.shape[0]
    small = [
        pltpu.make_async_copy(source, target, small_sem.at[at])
        for at, (source, target) in enumerate(((decay_hbm, dv), (b_hbm, bv), (c_hbm, cv)))
    ]

    def wide(group):
        lanes = pl.ds(pl.multiple_of(group * W, W), W)
        return (
            pltpu.make_async_copy(x_hbm.at[:, lanes], xv.at[group], wide_sem.at[0, group]),
            pltpu.make_async_copy(g_hbm.at[:, lanes], gv.at[group], wide_sem.at[1, group]),
        )

    for copy in small:
        copy.start()
    for group in range(G):
        for copy in wide(group):
            copy.start()
    barrier = pltpu.get_barrier_semaphore()
    for neighbour in (left, right):
        pl.semaphore_signal(barrier, inc=1, device_id=(pipe, neighbour), device_id_type=MESH)
    for copy in small:
        copy.wait()

    def states(group):
        for copy in wide(group):
            copy.wait()
        shape = (length, length)
        lower = ones_where(iota(shape, 1) <= iota(shape, 0))
        matrix = spread_matrix()
        decay = dv[pl.ds(pl.multiple_of(group * HPG, HPG), HPG), :]
        cum = columns_cumulative(decay * LOG2E, lower)
        lanes = pl.ds(pl.multiple_of(group * N, N), N)
        b = bv[:, lanes]
        c = cv[:, lanes]
        end = spread(jnp.exp2(cum[length - 1 : length, :] - cum), matrix)
        start = spread(jnp.exp2(cum), matrix)
        xw = (end * xv[group].astype(F32)).astype(BF16)
        gw = (start * gv[group].astype(F32)).astype(BF16)
        s = dot(b, xw, 0, 0)
        a = dot(c, gw, 0, 0)
        for k in range(halves):
            cut = slice(k * half, (k + 1) * half)
            s_ref[group * halves + k] = s[:, cut]
            a_ref[group * halves + k] = a[:, cut]
            e_ref[group * halves + k] = start[length - 1 : length, cut]

    def forward(k):
        return pltpu.make_async_remote_copy(
            src_ref=fs.at[k], dst_ref=ent_ref.at[k], send_sem=fsend.at[k], recv_sem=frecv.at[k],
            device_id=(pipe, right), device_id_type=MESH)

    def backward(k):
        return pltpu.make_async_remote_copy(
            src_ref=bs.at[k], dst_ref=adj_ref.at[k], send_sem=bsend.at[k], recv_sem=brecv.at[k],
            device_id=(pipe, left), device_id_type=MESH)

    def advance(k, place, make, got, local, sent):
        @pl.when(place > 0)
        def _():
            make(k).wait_recv()

        @pl.when(place == 0)
        def _():
            got[k] = jnp.zeros(got.shape[1:], BF16)

        @pl.when(place < n - 1)
        def _():
            sent[k] = (e_ref[k] * got[k].astype(F32) + local[k]).astype(BF16)
            make(k).start()

    def step(t, carry):
        kf = t - me
        kb = t - (n - 1 - me)

        @pl.when(jnp.logical_and(lax.rem(t, halves) == 0, t < PIECES))
        def _():
            states(lax.div(t, halves))

        @pl.when(t == 0)
        def _():
            pl.semaphore_wait(barrier, 2)

        @pl.when(jnp.logical_and(kf >= 0, kf < PIECES))
        def _():
            advance(kf, me, forward, ent_ref, s_ref, fs)

        @pl.when(jnp.logical_and(kb >= 0, kb < PIECES))
        def _():
            advance(kb, n - 1 - me, backward, adj_ref, a_ref, bs)

        return carry

    lax.fori_loop(0, n + PIECES - 1, step, 0)

    @pl.when(me < n - 1)
    def _():
        for k in range(PIECES):
            forward(k).wait_send()

    @pl.when(me > 0)
    def _():
        for k in range(PIECES):
            backward(k).wait_send()


def group_kernel(with_x, x_ref, b_ref, c_ref, decay_ref, g_ref, skip_ref, ent_ref, adj_ref, *refs):
    if with_x:
        gx_ref, *refs = refs
    (db_ref, dc_ref, gd_ref, xw_ref, gw_ref, end_ref, es_ref, ds_ref, edge_ref, cq_ref, cqt_ref, mixed_ref, row_ref, col_ref) = refs
    chunks = x_ref.shape[0] // Q
    square = (Q, Q)
    lower = ones_where(iota(square, 1) <= iota(square, 0))
    upper = ones_where(iota(square, 0) <= iota(square, 1))
    matrix = spread_matrix()
    half = ent_ref.shape[2]

    for k in range(W // half):
        es_ref[0, :, k * half : (k + 1) * half] = ent_ref[k]
        ds_ref[chunks - 1, :, k * half : (k + 1) * half] = adj_ref[k]
    col_ref[...] = jnp.zeros(square, F32)
    keep = []
    for c in range(chunks):
        rows = slice(c * Q, (c + 1) * Q)
        decay = decay_ref[:, rows] * LOG2E
        cum = columns_cumulative(decay, lower)
        cqt_ref[c] = cum
        cq_ref[c] = sum(dot(part, upper) for part in split3(decay))
        end = spread(jnp.exp2(cum[Q - 1 : Q, :] - cum), matrix)
        start = spread(jnp.exp2(cum), matrix)
        end_ref[rows, :] = end
        xw_ref[rows, :] = (end * x_ref[rows, :].astype(F32)).astype(BF16)
        gw_ref[rows, :] = (start * g_ref[rows, :].astype(F32)).astype(BF16)
        keep.append(start[Q - 1 : Q, :])
    for c in range(chunks - 1):
        rows = slice(c * Q, (c + 1) * Q)
        local = dot(b_ref[rows, :], xw_ref[rows, :], 0, 0)
        es_ref[c + 1] = (keep[c] * es_ref[c].astype(F32) + local).astype(BF16)
    for c in range(chunks - 1, 0, -1):
        rows = slice(c * Q, (c + 1) * Q)
        local = dot(c_ref[rows, :], gw_ref[rows, :], 0, 0)
        ds_ref[c - 1] = (keep[c] * ds_ref[c].astype(F32) + local).astype(BF16)

    def chunk(c, carry):
        rows = pl.ds(pl.multiple_of(c * Q, Q), Q)
        bc = b_ref[rows, :]
        cc = c_ref[rows, :]
        valid = iota(square, 1) >= iota(square, 0)
        inner = jnp.where(valid, dot(bc, cc, 1, 1), 0.0)
        edge_ref[...] = dot(bc, ds_ref[c])
        cqt = cqt_ref[c]
        low_lane = iota(square, 1) < P_SIZE
        for pair in range(HPG // 2):
            lanes = slice(pair * 128, (pair + 1) * 128)
            xp = x_ref[rows, lanes]
            gp = g_ref[rows, lanes]
            zero = jnp.zeros_like(gp)
            gm = jnp.concatenate([jnp.where(low_lane, gp, zero), jnp.where(low_lane, zero, gp)], axis=0)
            pair_prod = dot(xp, gm, 1, 1)
            inners = []
            mixed = None
            for i in range(2):
                h = 2 * pair + i
                gap = jnp.minimum(cq_ref[c, h : h + 1, :] - cqt[:, h : h + 1], 0.0)
                kernel = jnp.exp2(gap)
                kp = kernel * pair_prod[:, i * Q : (i + 1) * Q]
                mixed = kp if mixed is None else mixed + kp
                if with_x:
                    inners.append((kernel * inner).astype(BF16))
                joint = kp * inner
                row_ref[h : h + 1, :] = jnp.sum(joint, axis=0, keepdims=True)
                col_ref[:, h : h + 1] = jnp.sum(joint, axis=1, keepdims=True)
            if pair == 0:
                mixed_ref[...] = mixed
            else:
                mixed_ref[...] += mixed
            if not with_x:
                continue
            local = dot(jnp.concatenate(inners, axis=1), gm)
            gx_ref[rows, lanes] = (
                local + end_ref[rows, lanes] * edge_ref[:, lanes] + skip_ref[:, lanes] * gp.astype(F32)
            ).astype(BF16)
        mixed_t = jnp.where(valid, mixed_ref[...], 0.0)
        xw = xw_ref[rows, :]
        gw = gw_ref[rows, :]
        ent = es_ref[c]
        adj = ds_ref[c]
        db_ref[rows, :] = (dot(mixed_t.astype(BF16), cc) + dot(xw, adj, 1, 1)).astype(BF16)
        dc_ref[rows, :] = (dot(mixed_t.T.astype(BF16), bc) + dot(gw, ent, 1, 1)).astype(BF16)
        right = xw.astype(F32) * edge_ref[...]
        left = gw.astype(F32) * dot(cc, ent)
        both = left - right
        high = both.astype(BF16)
        low = (both - high.astype(F32)).astype(BF16)
        heads = ones_where(iota((HPG, W), 0) == iota((HPG, W), 1) // P_SIZE)
        terms = dot(heads, high, 1, 1) + dot(heads, low, 1, 1)
        total = jnp.exp2(cq_ref[c][:, Q - 1 : Q])
        cross = jnp.sum(ent.astype(F32) * adj.astype(F32), axis=0, keepdims=True)
        rights = jnp.sum(right, axis=0, keepdims=True)
        wide = heads.astype(F32)
        last = total * jnp.sum(wide * cross, axis=1, keepdims=True) + jnp.sum(wide * rights, axis=1, keepdims=True)
        grads = row_ref[...] - col_ref[...].T[:HPG, :] + terms
        grads = grads + jnp.where(iota((HPG, Q), 1) == Q - 1, last, 0.0)
        gd_ref[c] = sum(dot(part, lower) for part in split3(grads))
        return carry

    lax.fori_loop(0, chunks, chunk, 0)


def pack_kernel(heads, g_ref, b_ref, c_ref, decay_ref, skip_ref, raw_ref, out_ref, sems):
    g_lanes, b_lanes = heads * P_SIZE, heads // HPG * N
    copies = [
        pltpu.make_async_copy(g_ref.at[:, :g_lanes], raw_ref.at[:, :g_lanes], sems.at[0]),
        pltpu.make_async_copy(b_ref.at[:, :b_lanes], raw_ref.at[:, pl.ds(g_lanes, b_lanes)], sems.at[1]),
        pltpu.make_async_copy(c_ref.at[:, :b_lanes], raw_ref.at[:, pl.ds(g_lanes + b_lanes, b_lanes)], sems.at[2]),
    ]
    for copy in copies:
        copy.start()
    length = decay_ref.shape[1]
    out_ref[:, :length] = decay_ref[:heads, :]
    own = iota((heads, H), 0) == iota((heads, H), 1)
    column = jnp.sum(jnp.where(own, skip_ref[...], 0.0), axis=1, keepdims=True)
    out_ref[:, length:] = jnp.broadcast_to(column, (heads, 128))
    for copy in copies:
        copy.wait()


def passed_kernel(g_ref, b_ref, c_ref, decay_ref, adj_ref, gx_ref, gw_ref, end_ref, ds_ref, edge_ref, cq_ref, cqt_ref):
    length = g_ref.shape[0]
    chunks = length // Q
    square = (Q, Q)
    lower = ones_where(iota(square, 1) <= iota(square, 0))
    upper = ones_where(iota(square, 0) <= iota(square, 1))
    matrix = spread_matrix()
    half = adj_ref.shape[2]
    for k in range(W // half):
        ds_ref[chunks - 1, :, k * half : (k + 1) * half] = adj_ref[k]
    wide = ones_where(iota((HPG, W), 0) == iota((HPG, W), 1) // P_SIZE).astype(F32)
    skip = jnp.sum(wide * decay_ref[:, length : length + 1], axis=0, keepdims=True)
    keep = []
    for c in range(chunks):
        rows = slice(c * Q, (c + 1) * Q)
        decay = decay_ref[:, rows] * LOG2E
        cum = columns_cumulative(decay, lower)
        cqt_ref[c] = cum
        cq_ref[c] = sum(dot(part, upper) for part in split3(decay))
        end_ref[rows, :] = spread(jnp.exp2(cum[Q - 1 : Q, :] - cum), matrix)
        start = spread(jnp.exp2(cum), matrix)
        gw_ref[rows, :] = (start * g_ref[rows, :].astype(F32)).astype(BF16)
        keep.append(start[Q - 1 : Q, :])
    for c in range(chunks - 1, 0, -1):
        rows = slice(c * Q, (c + 1) * Q)
        local = dot(c_ref[rows, :], gw_ref[rows, :], 0, 0)
        ds_ref[c - 1] = (keep[c] * ds_ref[c].astype(F32) + local).astype(BF16)

    def chunk(c, carry):
        rows = pl.ds(pl.multiple_of(c * Q, Q), Q)
        bc = b_ref[rows, :]
        valid = iota(square, 1) >= iota(square, 0)
        inner = jnp.where(valid, dot(bc, c_ref[rows, :], 1, 1), 0.0)
        edge_ref[...] = dot(bc, ds_ref[c])
        cqt = cqt_ref[c]
        low_lane = iota(square, 1) < P_SIZE
        for pair in range(HPG // 2):
            lanes = slice(pair * 128, (pair + 1) * 128)
            gp = g_ref[rows, lanes]
            zero = jnp.zeros_like(gp)
            gm = jnp.concatenate([jnp.where(low_lane, gp, zero), jnp.where(low_lane, zero, gp)], axis=0)
            inners = []
            for i in range(2):
                h = 2 * pair + i
                gap = jnp.minimum(cq_ref[c, h : h + 1, :] - cqt[:, h : h + 1], 0.0)
                inners.append((jnp.exp2(gap) * inner).astype(BF16))
            local = dot(jnp.concatenate(inners, axis=1), gm)
            gx_ref[rows, lanes] = (
                local + end_ref[rows, lanes] * edge_ref[:, lanes] + skip[:, lanes] * gp.astype(F32)
            ).astype(BF16)
        return carry

    lax.fori_loop(0, chunks, chunk, 0)


def local(ssm_input, input_proj, output_proj, log_decay, grad_output, skip_gain):
    x, b, c, decay, g = ssm_input[0], input_proj[0], output_proj[0], log_decay[0], grad_output[0]
    length = x.shape[0]
    chunks = length // Q
    n = lax.axis_size("ctx")
    half = G * W // PIECES
    halves = W // half
    skip = jnp.repeat(skip_gain, P_SIZE, axis=1)
    devices = lax.axis_size("pipe")
    route = [(source, (source - 1) % devices) for source in range(devices)]

    def send(value):
        return lax.ppermute(value, "pipe", route)

    heads = RAW * HPG
    whole = pl.BlockSpec(memory_space=pltpu.VMEM)
    away = pl.BlockSpec(memory_space=pl.ANY)
    raw, raw_decay = pl.pallas_call(
        functools.partial(pack_kernel, heads),
        in_specs=[away] * 3 + [whole] * 2,
        out_specs=[away, whole],
        out_shape=[
            jax.ShapeDtypeStruct((length, heads * P_SIZE + 2 * RAW * N), BF16),
            jax.ShapeDtypeStruct((heads, length + 128), F32),
        ],
        scratch_shapes=[pltpu.SemaphoreType.DMA((3,))],
        compiler_params=pltpu.CompilerParams(vmem_limit_bytes=60 << 20),
        name="pack_raw",
    )(g, b, c, decay, skip_gain)
    raw = send(raw)
    raw_decay = send(raw_decay)

    states = jax.ShapeDtypeStruct((PIECES, N, half), BF16)
    entering, adjoint = pl.pallas_call(
        functools.partial(relay_kernel, n, halves, half),
        in_specs=[away] * 5,
        out_specs=[whole] * 2,
        out_shape=[states, states],
        scratch_shapes=[
            pltpu.VMEM((G, length, W), BF16),
            pltpu.VMEM((length, G * N), BF16),
            pltpu.VMEM((length, G * N), BF16),
            pltpu.VMEM((H, length), F32),
            pltpu.VMEM((G, length, W), BF16),
            pltpu.VMEM((PIECES, N, half), F32),
            pltpu.VMEM((PIECES, N, half), F32),
            pltpu.VMEM((PIECES, 1, half), F32),
            pltpu.VMEM((PIECES, N, half), BF16),
            pltpu.VMEM((PIECES, N, half), BF16),
            pltpu.SemaphoreType.DMA((3,)),
            pltpu.SemaphoreType.DMA((2, G)),
        ] + [pltpu.SemaphoreType.DMA((PIECES,))] * 4,
        compiler_params=pltpu.CompilerParams(collective_id=0, has_side_effects=True, vmem_limit_bytes=60 << 20),
        cost_estimate=pl.CostEstimate(flops=30_000_000_000, bytes_accessed=8_000_000, transcendentals=1_000_000),
        name="relay",
    )(x, b, c, decay, g)
    raw_adjoint = send(adjoint[: RAW * halves])

    def own_group(group, with_x):
        pick = lambda i: (0, group)
        rows = lambda i: (group, 0)
        pieces = pl.BlockSpec((halves, N, half), lambda i: (group, 0, 0))
        flat = lambda i: (0, 0)
        out_specs = [
            pl.BlockSpec((length, W), flat),
            pl.BlockSpec((length, N), flat),
            pl.BlockSpec((length, N), flat),
            pl.BlockSpec((chunks, HPG, Q), lambda i: (0, 0, 0)),
        ]
        out_shape = [
            jax.ShapeDtypeStruct((length, W), BF16),
            jax.ShapeDtypeStruct((length, N), BF16),
            jax.ShapeDtypeStruct((length, N), BF16),
            jax.ShapeDtypeStruct((chunks, HPG, Q), F32),
        ]
        first = 0 if with_x else 1
        return pl.pallas_call(
            functools.partial(group_kernel, with_x),
            grid=(1,),
            in_specs=[
                pl.BlockSpec((length, W), pick),
                pl.BlockSpec((length, N), pick),
                pl.BlockSpec((length, N), pick),
                pl.BlockSpec((HPG, length), rows),
                pl.BlockSpec((length, W), pick),
                pl.BlockSpec((1, W), pick),
                pieces,
                pieces,
            ],
            out_specs=out_specs[first:],
            out_shape=out_shape[first:],
            scratch_shapes=[
                pltpu.VMEM((length, W), BF16),
                pltpu.VMEM((length, W), BF16),
                pltpu.VMEM((length, W), F32),
                pltpu.VMEM((chunks, N, W), BF16),
                pltpu.VMEM((chunks, N, W), BF16),
                pltpu.VMEM((Q, W), F32),
                pltpu.VMEM((chunks, HPG, Q), F32),
                pltpu.VMEM((chunks, Q, 2 * HPG), F32),
                pltpu.VMEM((Q, Q), F32),
                pltpu.VMEM((HPG, Q), F32),
                pltpu.VMEM((Q, Q), F32),
            ],
            compiler_params=pltpu.CompilerParams(vmem_limit_bytes=60 << 20),
            cost_estimate=pl.CostEstimate(flops=3_000_000_000, bytes_accessed=4_000_000, transcendentals=1_000_000),
            name="group_grads",
        )(x, b, c, decay, g, skip, entering, adjoint)

    sent = {}
    rest = {}
    for group in list(range(RAW, G)) + list(range(RAW)):
        out = own_group(group, group >= RAW)
        if group >= RAW:
            sent[group] = send(out[0])
        rest[group] = out[-3:]
    passed_first = pl.pallas_call(
        passed_kernel,
        grid=(RAW,),
        in_specs=[
            pl.BlockSpec((length, W), lambda i: (0, i)),
            pl.BlockSpec((length, N), lambda i: (0, RAW * (W // N) + i)),
            pl.BlockSpec((length, N), lambda i: (0, RAW * (W // N) + RAW + i)),
            pl.BlockSpec((HPG, length + 128), lambda i: (i, 0)),
            pl.BlockSpec((halves, N, half), lambda i: (i, 0, 0)),
        ],
        out_specs=pl.BlockSpec((length, W), lambda i: (0, i)),
        out_shape=jax.ShapeDtypeStruct((length, RAW * W), BF16),
        scratch_shapes=[
            pltpu.VMEM((length, W), BF16),
            pltpu.VMEM((length, W), F32),
            pltpu.VMEM((chunks, N, W), BF16),
            pltpu.VMEM((Q, W), F32),
            pltpu.VMEM((chunks, HPG, Q), F32),
            pltpu.VMEM((chunks, Q, 2 * HPG), F32),
        ],
        compiler_params=pltpu.CompilerParams(vmem_limit_bytes=60 << 20),
        cost_estimate=pl.CostEstimate(flops=4_000_000_000, bytes_accessed=4_000_000, transcendentals=1_000_000),
        name="passed_grads",
    )(raw, raw, raw, raw_decay, raw_adjoint)
    grad_x = jnp.concatenate([passed_first] + [sent[group] for group in range(RAW, G)], axis=1)
    grad_b = jnp.concatenate([rest[group][0] for group in range(G)], axis=1)
    grad_c = jnp.concatenate([rest[group][1] for group in range(G)], axis=1)
    grad_decay = jnp.concatenate([rest[group][2].transpose(1, 0, 2).reshape(HPG, length) for group in range(G)], axis=0)
    return grad_x[None], grad_b[None], grad_c[None], grad_decay[None]


def solution(mesh):
    return jax.shard_map(
        local,
        mesh=mesh,
        in_specs=(
            P("pipe", "ctx", None),
            P("pipe", "ctx", None),
            P("pipe", "ctx", None),
            P("pipe", None, "ctx"),
            P("pipe", "ctx", None),
            P("pipe", None),
        ),
        out_specs=(
            P("pipe", "ctx", None),
            P("pipe", "ctx", None),
            P("pipe", "ctx", None),
            P("pipe", None, "ctx"),
        ),
        check_vma=False,
    )
```

```python
import functools

import jax
import jax.numpy as jnp
from jax import lax
from jax.experimental import pallas as pl
from jax.experimental.pallas import tpu as pltpu
from jax.sharding import PartitionSpec as P

H = 64
P_SIZE = 64
N = 128
G = 4
HPG = 16
W = HPG * P_SIZE
Q = 128
PIECES = 8
RAW = 2
LOG2E = 1.4426950408889634
MESH = pl.DeviceIdType.MESH
F32 = jnp.float32
BF16 = jnp.bfloat16


def dot(a, b, ca=1, cb=0):
    return lax.dot_general(a, b, (((ca,), (cb,)), ((), ())), preferred_element_type=F32)


def iota(shape, axis):
    return lax.broadcasted_iota(jnp.int32, shape, axis)


def split3(value):
    high = value.astype(BF16)
    rest = value - high.astype(F32)
    middle = rest.astype(BF16)
    return high, middle, (rest - middle.astype(F32)).astype(BF16)


def ones_where(condition):
    return jnp.where(condition, 1.0, 0.0).astype(BF16)


def spread_matrix():
    shape = (2 * HPG, W)
    return ones_where(iota(shape, 0) % HPG == iota(shape, 1) // P_SIZE)


def spread(weights, matrix):
    high = weights.astype(BF16)
    low = (weights - high.astype(F32)).astype(BF16)
    first = iota(weights.shape, 1) < HPG
    return dot(jnp.where(first, high.astype(F32), low.astype(F32)).astype(BF16), matrix)


def columns_cumulative(decay, lower):
    twice = jnp.concatenate([decay, decay], axis=0)
    return sum(dot(lower, part, 1, 1) for part in split3(twice))


def relay_kernel(n, halves, half, x_hbm, b_hbm, c_hbm, decay_hbm, g_hbm, ent_ref, adj_ref, gx_ref, db_ref, dc_ref, diff_ref,
                 mixed_ref, row_ref, col_ref, xv, bv, cv, dv, gv, s_ref, a_ref, e_ref, fs, bs, small_sem, wide_sem, fsend, frecv, bsend, brecv):
    me = lax.axis_index("ctx")
    pipe = lax.axis_index("pipe")
    right, left = lax.rem(me + 1, n), lax.rem(me + n - 1, n)
    length = x_hbm.shape[0]
    small = [
        pltpu.make_async_copy(source, target, small_sem.at[at])
        for at, (source, target) in enumerate(((decay_hbm, dv), (b_hbm, bv), (c_hbm, cv)))
    ]

    def wide(group):
        lanes = pl.ds(pl.multiple_of(group * W, W), W)
        return (
            pltpu.make_async_copy(x_hbm.at[:, lanes], xv.at[group], wide_sem.at[0, group]),
            pltpu.make_async_copy(g_hbm.at[:, lanes], gv.at[group], wide_sem.at[1, group]),
        )

    for copy in small:
        copy.start()
    for group in range(G):
        for copy in wide(group):
            copy.start()
    barrier = pltpu.get_barrier_semaphore()
    for neighbour in (left, right):
        pl.semaphore_signal(barrier, inc=1, device_id=(pipe, neighbour), device_id_type=MESH)
    for copy in small:
        copy.wait()

    def states(group):
        for copy in wide(group):
            copy.wait()
        shape = (length, length)
        lower = ones_where(iota(shape, 1) <= iota(shape, 0))
        matrix = spread_matrix()
        decay = dv[pl.ds(pl.multiple_of(group * HPG, HPG), HPG), :]
        cum = columns_cumulative(decay * LOG2E, lower)
        lanes = pl.ds(pl.multiple_of(group * N, N), N)
        b = bv[:, lanes]
        c = cv[:, lanes]
        end = spread(jnp.exp2(cum[length - 1 : length, :] - cum), matrix)
        start = spread(jnp.exp2(cum), matrix)
        xw = (end * xv[group].astype(F32)).astype(BF16)
        gw = (start * gv[group].astype(F32)).astype(BF16)
        s = dot(b, xw, 0, 0)
        a = dot(c, gw, 0, 0)
        for k in range(halves):
            cut = slice(k * half, (k + 1) * half)
            s_ref[group * halves + k] = s[:, cut]
            a_ref[group * halves + k] = a[:, cut]
            e_ref[group * halves + k] = start[length - 1 : length, cut]

    chunks = length // Q
    col_ref[...] = jnp.zeros((Q, Q), F32)

    def unit(group, c):
        square = (Q, Q)
        lower = ones_where(iota(square, 1) <= iota(square, 0))
        upper = ones_where(iota(square, 0) <= iota(square, 1))
        rows = pl.ds(pl.multiple_of(c * Q, Q), Q)
        lanes_n = pl.ds(pl.multiple_of(group * N, N), N)
        decay = dv[pl.ds(pl.multiple_of(group * HPG, HPG), HPG), rows] * LOG2E
        cqt = columns_cumulative(decay, lower)
        cq = sum(dot(part, upper) for part in split3(decay))
        bc = bv[rows, lanes_n]
        cc = cv[rows, lanes_n]
        valid = iota(square, 1) >= iota(square, 0)
        inner = jnp.where(valid, dot(bc, cc, 1, 1), 0.0)
        low_lane = iota(square, 1) < P_SIZE
        for pair in range(HPG // 2):
            lanes = slice(pair * 128, (pair + 1) * 128)
            xp = xv[group, rows, lanes]
            gp = gv[group, rows, lanes]
            zero = jnp.zeros_like(gp)
            gm = jnp.concatenate([jnp.where(low_lane, gp, zero), jnp.where(low_lane, zero, gp)], axis=0)
            pair_prod = dot(xp, gm, 1, 1)
            inners = []
            mixed = None
            for i in range(2):
                h = 2 * pair + i
                kernel = jnp.exp2(jnp.minimum(cq[h : h + 1, :] - cqt[:, h : h + 1], 0.0))
                kp = kernel * pair_prod[:, i * Q : (i + 1) * Q]
                mixed = kp if mixed is None else mixed + kp
                inners.append((kernel * inner).astype(BF16))
                joint = kp * inner
                row_ref[h : h + 1, :] = jnp.sum(joint, axis=0, keepdims=True)
                col_ref[:, h : h + 1] = jnp.sum(joint, axis=1, keepdims=True)
            if pair == 0:
                mixed_ref[...] = mixed
            else:
                mixed_ref[...] += mixed
            gx_ref[group, rows, lanes] = dot(jnp.concatenate(inners, axis=1), gm).astype(BF16)
        mixed_t = jnp.where(valid, mixed_ref[...], 0.0)
        db_ref[rows, lanes_n] = dot(mixed_t.astype(BF16), cc)
        dc_ref[rows, lanes_n] = dot(mixed_t.T.astype(BF16), bc)
        diff_ref[group * chunks + c] = row_ref[...] - col_ref[...].T[:HPG, :]

    def forward(k):
        return pltpu.make_async_remote_copy(
            src_ref=fs.at[k], dst_ref=ent_ref.at[k], send_sem=fsend.at[k], recv_sem=frecv.at[k],
            device_id=(pipe, right), device_id_type=MESH)

    def backward(k):
        return pltpu.make_async_remote_copy(
            src_ref=bs.at[k], dst_ref=adj_ref.at[k], send_sem=bsend.at[k], recv_sem=brecv.at[k],
            device_id=(pipe, left), device_id_type=MESH)

    def advance(k, place, make, got, local, sent):
        @pl.when(place > 0)
        def _():
            make(k).wait_recv()

        @pl.when(place == 0)
        def _():
            got[k] = jnp.zeros(got.shape[1:], BF16)

        @pl.when(place < n - 1)
        def _():
            sent[k] = (e_ref[k] * got[k].astype(F32) + local[k]).astype(BF16)
            make(k).start()

    def step(t, carry):
        kf = t - me
        kb = t - (n - 1 - me)

        @pl.when(jnp.logical_and(lax.rem(t, halves) == 0, t < PIECES))
        def _():
            states(lax.div(t, halves))

        @pl.when(t == 0)
        def _():
            pl.semaphore_wait(barrier, 2)

        @pl.when(jnp.logical_and(kf >= 0, kf < PIECES))
        def _():
            advance(kf, me, forward, ent_ref, s_ref, fs)

        @pl.when(jnp.logical_and(kb >= 0, kb < PIECES))
        def _():
            advance(kb, n - 1 - me, backward, adj_ref, a_ref, bs)

        @pl.when(t < G * chunks)
        def _():
            unit(lax.div(t, chunks), lax.rem(t, chunks))

        return carry

    lax.fori_loop(0, max(n + PIECES - 1, G * chunks), step, 0)

    @pl.when(me < n - 1)
    def _():
        for k in range(PIECES):
            forward(k).wait_send()

    @pl.when(me > 0)
    def _():
        for k in range(PIECES):
            backward(k).wait_send()


def group_kernel(with_x, x_ref, b_ref, c_ref, decay_ref, g_ref, skip_ref, ent_ref, adj_ref,
                 near_db_ref, near_dc_ref, diff_ref, *refs):
    if with_x:
        near_gx_ref, gx_ref, *refs = refs
    db_ref, dc_ref, gd_ref, es_ref, ds_ref = refs
    chunks = x_ref.shape[0] // Q
    square = (Q, Q)
    lower = ones_where(iota(square, 1) <= iota(square, 0))
    matrix = spread_matrix()
    heads = ones_where(iota((HPG, W), 0) == iota((HPG, W), 1) // P_SIZE)
    wide = heads.astype(F32)
    half = ent_ref.shape[2]

    for k in range(W // half):
        es_ref[0, :, k * half : (k + 1) * half] = ent_ref[k]
        ds_ref[chunks - 1, :, k * half : (k + 1) * half] = adj_ref[k]
    spans = [slice(c * Q, (c + 1) * Q) for c in range(chunks)]
    ends, xws, gws, keep = [], [], [], []
    for rows in spans:
        cum = columns_cumulative(decay_ref[:, rows] * LOG2E, lower)
        end = spread(jnp.exp2(cum[Q - 1 : Q, :] - cum), matrix)
        start = spread(jnp.exp2(cum), matrix)
        ends.append(end)
        xws.append((end * x_ref[rows, :].astype(F32)).astype(BF16))
        gws.append((start * g_ref[rows, :].astype(F32)).astype(BF16))
        keep.append(start[Q - 1 : Q, :])
    for c in range(chunks - 1):
        near = dot(b_ref[spans[c], :], xws[c], 0, 0)
        es_ref[c + 1] = (keep[c] * es_ref[c].astype(F32) + near).astype(BF16)
    for c in range(chunks - 1, 0, -1):
        near = dot(c_ref[spans[c], :], gws[c], 0, 0)
        ds_ref[c - 1] = (keep[c] * ds_ref[c].astype(F32) + near).astype(BF16)
    for c, rows in enumerate(spans):
        ent = es_ref[c]
        adj = ds_ref[c]
        edge = dot(b_ref[rows, :], adj)
        if with_x:
            gx_ref[rows, :] = (
                near_gx_ref[0, rows, :].astype(F32) + ends[c] * edge + skip_ref[...] * g_ref[rows, :].astype(F32)
            ).astype(BF16)
        db_ref[rows, :] = (near_db_ref[rows, :] + dot(xws[c], adj, 1, 1)).astype(BF16)
        dc_ref[rows, :] = (near_dc_ref[rows, :] + dot(gws[c], ent, 1, 1)).astype(BF16)
        right = xws[c].astype(F32) * edge
        left = gws[c].astype(F32) * dot(c_ref[rows, :], ent)
        both = left - right
        high = both.astype(BF16)
        low = (both - high.astype(F32)).astype(BF16)
        terms = dot(heads, high, 1, 1) + dot(heads, low, 1, 1)
        cross = keep[c] * jnp.sum(ent.astype(F32) * adj.astype(F32), axis=0, keepdims=True)
        rights = jnp.sum(right, axis=0, keepdims=True)
        last = jnp.sum(wide * (cross + rights), axis=1, keepdims=True)
        grads = diff_ref[c] + terms
        grads = grads + jnp.where(iota((HPG, Q), 1) == Q - 1, last, 0.0)
        gd_ref[:, rows] = sum(dot(part, lower) for part in split3(grads))


def pack_kernel(heads, g_ref, b_ref, c_ref, decay_ref, skip_ref, raw_ref, out_ref):
    g_lanes, b_lanes = heads * P_SIZE, heads // HPG * N
    raw_ref[:, :g_lanes] = g_ref[...]
    raw_ref[:, g_lanes : g_lanes + b_lanes] = b_ref[...]
    raw_ref[:, g_lanes + b_lanes :] = c_ref[...]
    length = decay_ref.shape[1]
    out_ref[:, :length] = decay_ref[...]
    own = iota((heads, H), 0) == iota((heads, H), 1)
    column = jnp.sum(jnp.where(own, skip_ref[...], 0.0), axis=1, keepdims=True)
    out_ref[:, length:] = jnp.broadcast_to(column, (heads, 128))


def passed_kernel(g_ref, b_ref, c_ref, decay_ref, adj_ref, gx_ref, gw_ref, end_ref, ds_ref, edge_ref, cq_ref, cqt_ref):
    length = g_ref.shape[0]
    chunks = length // Q
    square = (Q, Q)
    lower = ones_where(iota(square, 1) <= iota(square, 0))
    upper = ones_where(iota(square, 0) <= iota(square, 1))
    matrix = spread_matrix()
    half = adj_ref.shape[2]
    for k in range(W // half):
        ds_ref[chunks - 1, :, k * half : (k + 1) * half] = adj_ref[k]
    wide = ones_where(iota((HPG, W), 0) == iota((HPG, W), 1) // P_SIZE).astype(F32)
    skip = jnp.sum(wide * decay_ref[:, length : length + 1], axis=0, keepdims=True)
    keep = []
    for c in range(chunks):
        rows = slice(c * Q, (c + 1) * Q)
        decay = decay_ref[:, rows] * LOG2E
        cum = columns_cumulative(decay, lower)
        cqt_ref[c] = cum
        cq_ref[c] = sum(dot(part, upper) for part in split3(decay))
        end_ref[rows, :] = spread(jnp.exp2(cum[Q - 1 : Q, :] - cum), matrix)
        start = spread(jnp.exp2(cum), matrix)
        gw_ref[rows, :] = (start * g_ref[rows, :].astype(F32)).astype(BF16)
        keep.append(start[Q - 1 : Q, :])
    for c in range(chunks - 1, 0, -1):
        rows = slice(c * Q, (c + 1) * Q)
        local = dot(c_ref[rows, :], gw_ref[rows, :], 0, 0)
        ds_ref[c - 1] = (keep[c] * ds_ref[c].astype(F32) + local).astype(BF16)

    def chunk(c, carry):
        rows = pl.ds(pl.multiple_of(c * Q, Q), Q)
        bc = b_ref[rows, :]
        valid = iota(square, 1) >= iota(square, 0)
        inner = jnp.where(valid, dot(bc, c_ref[rows, :], 1, 1), 0.0)
        edge_ref[...] = dot(bc, ds_ref[c])
        cqt = cqt_ref[c]
        low_lane = iota(square, 1) < P_SIZE
        for pair in range(HPG // 2):
            lanes = slice(pair * 128, (pair + 1) * 128)
            gp = g_ref[rows, lanes]
            zero = jnp.zeros_like(gp)
            gm = jnp.concatenate([jnp.where(low_lane, gp, zero), jnp.where(low_lane, zero, gp)], axis=0)
            inners = []
            for i in range(2):
                h = 2 * pair + i
                gap = jnp.minimum(cq_ref[c, h : h + 1, :] - cqt[:, h : h + 1], 0.0)
                inners.append((jnp.exp2(gap) * inner).astype(BF16))
            local = dot(jnp.concatenate(inners, axis=1), gm)
            gx_ref[rows, lanes] = (
                local + end_ref[rows, lanes] * edge_ref[:, lanes] + skip[:, lanes] * gp.astype(F32)
            ).astype(BF16)
        return carry

    lax.fori_loop(0, chunks, chunk, 0)


def local(ssm_input, input_proj, output_proj, log_decay, grad_output, skip_gain):
    x, b, c, decay, g = ssm_input[0], input_proj[0], output_proj[0], log_decay[0], grad_output[0]
    length = x.shape[0]
    chunks = length // Q
    n = lax.axis_size("ctx")
    half = G * W // PIECES
    halves = W // half
    skip = jnp.repeat(skip_gain, P_SIZE, axis=1)
    devices = lax.axis_size("pipe")
    route = [(source, (source - 1) % devices) for source in range(devices)]

    def send(value):
        return lax.ppermute(value, "pipe", route)

    heads = RAW * HPG
    whole = pl.BlockSpec(memory_space=pltpu.VMEM)
    away = pl.BlockSpec(memory_space=pl.ANY)
    raw, raw_decay = pl.pallas_call(
        functools.partial(pack_kernel, heads),
        grid=(1,),
        in_specs=[
            pl.BlockSpec((length, RAW * W), lambda i: (0, 0)),
            pl.BlockSpec((length, RAW * N), lambda i: (0, 0)),
            pl.BlockSpec((length, RAW * N), lambda i: (0, 0)),
            pl.BlockSpec((heads, length), lambda i: (0, 0)),
            pl.BlockSpec((1, H), lambda i: (0, 0)),
        ],
        out_specs=[
            pl.BlockSpec((length, heads * P_SIZE + 2 * RAW * N), lambda i: (0, 0)),
            pl.BlockSpec((heads, length + 128), lambda i: (0, 0)),
        ],
        out_shape=[
            jax.ShapeDtypeStruct((length, heads * P_SIZE + 2 * RAW * N), BF16),
            jax.ShapeDtypeStruct((heads, length + 128), F32),
        ],
        compiler_params=pltpu.CompilerParams(vmem_limit_bytes=60 << 20),
        name="pack_raw",
    )(g, b, c, decay, skip_gain)
    raw = send(raw)
    raw_decay = send(raw_decay)

    states = jax.ShapeDtypeStruct((PIECES, N, half), BF16)
    entering, adjoint, near_gx, near_db, near_dc, diff = pl.pallas_call(
        functools.partial(relay_kernel, n, halves, half),
        in_specs=[away] * 5,
        out_specs=[whole] * 6,
        out_shape=[
            states,
            states,
            jax.ShapeDtypeStruct((G, length, W), BF16),
            jax.ShapeDtypeStruct((length, G * N), F32),
            jax.ShapeDtypeStruct((length, G * N), F32),
            jax.ShapeDtypeStruct((G * chunks, HPG, Q), F32),
        ],
        scratch_shapes=[
            pltpu.VMEM((Q, Q), F32),
            pltpu.VMEM((HPG, Q), F32),
            pltpu.VMEM((Q, Q), F32),
            pltpu.VMEM((G, length, W), BF16),
            pltpu.VMEM((length, G * N), BF16),
            pltpu.VMEM((length, G * N), BF16),
            pltpu.VMEM((H, length), F32),
            pltpu.VMEM((G, length, W), BF16),
            pltpu.VMEM((PIECES, N, half), F32),
            pltpu.VMEM((PIECES, N, half), F32),
            pltpu.VMEM((PIECES, 1, half), F32),
            pltpu.VMEM((PIECES, N, half), BF16),
            pltpu.VMEM((PIECES, N, half), BF16),
            pltpu.SemaphoreType.DMA((3,)),
            pltpu.SemaphoreType.DMA((2, G)),
        ] + [pltpu.SemaphoreType.DMA((PIECES,))] * 4,
        compiler_params=pltpu.CompilerParams(collective_id=0, has_side_effects=True, vmem_limit_bytes=60 << 20),
        cost_estimate=pl.CostEstimate(flops=30_000_000_000, bytes_accessed=8_000_000, transcendentals=1_000_000),
        name="relay",
    )(x, b, c, decay, g)
    raw_adjoint = send(adjoint[: RAW * halves])

    def own_group(group, with_x):
        pick = lambda i: (0, group)
        rows = lambda i: (group, 0)
        pieces = pl.BlockSpec((halves, N, half), lambda i: (group, 0, 0))
        flat = lambda i: (0, 0)
        out_specs = [
            pl.BlockSpec((length, W), flat),
            pl.BlockSpec((length, N), flat),
            pl.BlockSpec((length, N), flat),
            pl.BlockSpec((HPG, length), flat),
        ]
        out_shape = [
            jax.ShapeDtypeStruct((length, W), BF16),
            jax.ShapeDtypeStruct((length, N), BF16),
            jax.ShapeDtypeStruct((length, N), BF16),
            jax.ShapeDtypeStruct((HPG, length), F32),
        ]
        first = 0 if with_x else 1
        return pl.pallas_call(
            functools.partial(group_kernel, with_x),
            grid=(1,),
            in_specs=[
                pl.BlockSpec((length, W), pick),
                pl.BlockSpec((length, N), pick),
                pl.BlockSpec((length, N), pick),
                pl.BlockSpec((HPG, length), rows),
                pl.BlockSpec((length, W), pick),
                pl.BlockSpec((1, W), pick),
                pieces,
                pieces,
                pl.BlockSpec((length, N), pick),
                pl.BlockSpec((length, N), pick),
                pl.BlockSpec((chunks, HPG, Q), lambda i: (group, 0, 0)),
            ] + [pl.BlockSpec((1, length, W), lambda i: (group, 0, 0))] * with_x,
            out_specs=out_specs[first:],
            out_shape=out_shape[first:],
            scratch_shapes=[pltpu.VMEM((chunks, N, W), BF16), pltpu.VMEM((chunks, N, W), BF16)],
            compiler_params=pltpu.CompilerParams(vmem_limit_bytes=60 << 20),
            cost_estimate=pl.CostEstimate(flops=3_000_000_000, bytes_accessed=4_000_000, transcendentals=1_000_000),
            name="group_grads",
        )(x, b, c, decay, g, skip, entering, adjoint, near_db, near_dc, diff, *[near_gx][: int(with_x)])

    sent = {}
    rest = {}
    for group in list(range(RAW, G)) + list(range(RAW)):
        out = own_group(group, group >= RAW)
        if group >= RAW:
            sent[group] = send(out[0])
        rest[group] = out[-3:]
    passed_first = pl.pallas_call(
        passed_kernel,
        grid=(RAW,),
        in_specs=[
            pl.BlockSpec((length, W), lambda i: (0, i)),
            pl.BlockSpec((length, N), lambda i: (0, RAW * (W // N) + i)),
            pl.BlockSpec((length, N), lambda i: (0, RAW * (W // N) + RAW + i)),
            pl.BlockSpec((HPG, length + 128), lambda i: (i, 0)),
            pl.BlockSpec((halves, N, half), lambda i: (i, 0, 0)),
        ],
        out_specs=pl.BlockSpec((length, W), lambda i: (0, i)),
        out_shape=jax.ShapeDtypeStruct((length, RAW * W), BF16),
        scratch_shapes=[
            pltpu.VMEM((length, W), BF16),
            pltpu.VMEM((length, W), F32),
            pltpu.VMEM((chunks, N, W), BF16),
            pltpu.VMEM((Q, W), F32),
            pltpu.VMEM((chunks, HPG, Q), F32),
            pltpu.VMEM((chunks, Q, 2 * HPG), F32),
        ],
        compiler_params=pltpu.CompilerParams(vmem_limit_bytes=60 << 20),
        cost_estimate=pl.CostEstimate(flops=4_000_000_000, bytes_accessed=4_000_000, transcendentals=1_000_000),
        name="passed_grads",
    )(raw, raw, raw, raw_decay, raw_adjoint)
    grad_x = jnp.concatenate([passed_first] + [sent[group] for group in range(RAW, G)], axis=1)
    grad_b = jnp.concatenate([rest[group][0] for group in range(G)], axis=1)
    grad_c = jnp.concatenate([rest[group][1] for group in range(G)], axis=1)
    grad_decay = jnp.concatenate([rest[group][2] for group in range(G)], axis=0)
    return grad_x[None], grad_b[None], grad_c[None], grad_decay[None]


def solution(mesh):
    return jax.shard_map(
        local,
        mesh=mesh,
        in_specs=(
            P("pipe", "ctx", None),
            P("pipe", "ctx", None),
            P("pipe", "ctx", None),
            P("pipe", None, "ctx"),
            P("pipe", "ctx", None),
            P("pipe", None),
        ),
        out_specs=(
            P("pipe", "ctx", None),
            P("pipe", "ctx", None),
            P("pipe", "ctx", None),
            P("pipe", None, "ctx"),
        ),
        check_vma=False,
    )
```

```python
import functools

import jax
import jax.numpy as jnp
from jax import lax
from jax.experimental import pallas as pl
from jax.experimental.pallas import tpu as pltpu
from jax.sharding import PartitionSpec as P

H = 64
P_SIZE = 64
N = 128
G = 4
HPG = 16
W = HPG * P_SIZE
Q = 128
PIECES = 8
SKEW = 2
RAW = 2
LOG2E = 1.4426950408889634
MESH = pl.DeviceIdType.MESH
F32 = jnp.float32
BF16 = jnp.bfloat16


def dot(a, b, ca=1, cb=0):
    return lax.dot_general(a, b, (((ca,), (cb,)), ((), ())), preferred_element_type=F32)


def iota(shape, axis):
    return lax.broadcasted_iota(jnp.int32, shape, axis)


def split3(value):
    high = value.astype(BF16)
    rest = value - high.astype(F32)
    middle = rest.astype(BF16)
    return high, middle, (rest - middle.astype(F32)).astype(BF16)


def ones_where(condition):
    return jnp.where(condition, 1.0, 0.0).astype(BF16)


def spread_matrix():
    shape = (2 * HPG, W)
    return ones_where(iota(shape, 0) % HPG == iota(shape, 1) // P_SIZE)


def spread(weights, matrix):
    high = weights.astype(BF16)
    low = (weights - high.astype(F32)).astype(BF16)
    first = iota(weights.shape, 1) < HPG
    return dot(jnp.where(first, high.astype(F32), low.astype(F32)).astype(BF16), matrix)


def columns_cumulative(decay, lower):
    twice = jnp.concatenate([decay, decay], axis=0)
    return sum(dot(lower, part, 1, 1) for part in split3(twice))


def relay_kernel(n, halves, half, x_hbm, b_hbm, c_hbm, decay_hbm, g_hbm, ent_ref, adj_ref, gx_ref, db_ref, dc_ref, diff_ref, first_adj_ref,
                 mixed_ref, row_ref, col_ref, xv, bv, cv, dv, gv, s_ref, a_ref, e_ref, fs, bs, small_sem, wide_sem, fsend, frecv, bsend, brecv):
    me = lax.axis_index("ctx")
    pipe = lax.axis_index("pipe")
    right, left = lax.rem(me + 1, n), lax.rem(me + n - 1, n)
    length = x_hbm.shape[0]
    small = [
        pltpu.make_async_copy(source, target, small_sem.at[at])
        for at, (source, target) in enumerate(((decay_hbm, dv), (b_hbm, bv), (c_hbm, cv)))
    ]

    def wide(group):
        lanes = pl.ds(pl.multiple_of(group * W, W), W)
        return (
            pltpu.make_async_copy(x_hbm.at[:, lanes], xv.at[group], wide_sem.at[0, group]),
            pltpu.make_async_copy(g_hbm.at[:, lanes], gv.at[group], wide_sem.at[1, group]),
        )

    for copy in small:
        copy.start()
    for group in range(G):
        for copy in wide(group):
            copy.start()
    barrier = pltpu.get_barrier_semaphore()
    for neighbour in (left, right):
        pl.semaphore_signal(barrier, inc=1, device_id=(pipe, neighbour), device_id_type=MESH)
    for copy in small:
        copy.wait()

    def states(group):
        for copy in wide(group):
            copy.wait()
        shape = (length, length)
        lower = ones_where(iota(shape, 1) <= iota(shape, 0))
        matrix = spread_matrix()
        decay = dv[pl.ds(pl.multiple_of(group * HPG, HPG), HPG), :]
        cum = columns_cumulative(decay * LOG2E, lower)
        lanes = pl.ds(pl.multiple_of(group * N, N), N)
        b = bv[:, lanes]
        c = cv[:, lanes]
        end = spread(jnp.exp2(cum[length - 1 : length, :] - cum), matrix)
        start = spread(jnp.exp2(cum), matrix)
        xw = (end * xv[group].astype(F32)).astype(BF16)
        gw = (start * gv[group].astype(F32)).astype(BF16)
        s = dot(b, xw, 0, 0)
        a = dot(c, gw, 0, 0)
        for k in range(halves):
            cut = slice(k * half, (k + 1) * half)
            s_ref[group * halves + k] = s[:, cut]
            a_ref[group * halves + k] = a[:, cut]
            e_ref[group * halves + k] = start[length - 1 : length, cut]

    chunks = length // Q
    col_ref[...] = jnp.zeros(col_ref.shape, F32)
    few = HPG // 2

    def unit(group, c, part):
        square = (Q, Q)
        lower = ones_where(iota(square, 1) <= iota(square, 0))
        upper = ones_where(iota(square, 0) <= iota(square, 1))
        rows = pl.ds(pl.multiple_of(c * Q, Q), Q)
        lanes_n = pl.ds(pl.multiple_of(group * N, N), N)
        pieces = split3(dv[pl.ds(pl.multiple_of(group * HPG + part * few, few), few), rows] * LOG2E)
        cqt = sum(dot(lower, piece, 1, 1) for piece in pieces)
        cq = sum(dot(piece, upper) for piece in pieces)
        bc = bv[rows, lanes_n]
        cc = cv[rows, lanes_n]
        valid = iota(square, 1) >= iota(square, 0)
        inner = jnp.where(valid, dot(bc, cc, 1, 1), 0.0)
        low_lane = iota(square, 1) < P_SIZE

        @pl.when(part == 0)
        def _():
            mixed_ref[...] = jnp.zeros(square, F32)

        for pair in range(few // 2):
            lanes = pl.ds(pl.multiple_of(part * (W // 2) + pair * 128, 128), 128)
            xp = xv[group, rows, lanes]
            gp = gv[group, rows, lanes]
            zero = jnp.zeros_like(gp)
            gm = jnp.concatenate([jnp.where(low_lane, gp, zero), jnp.where(low_lane, zero, gp)], axis=0)
            pair_prod = dot(xp, gm, 1, 1)
            inners = []
            mixed = None
            for i in range(2):
                h = 2 * pair + i
                kernel = jnp.exp2(jnp.minimum(cq[h : h + 1, :] - cqt[:, h : h + 1], 0.0))
                kp = kernel * pair_prod[:, i * Q : (i + 1) * Q]
                mixed = kp if mixed is None else mixed + kp
                inners.append((kernel * inner).astype(BF16))
                joint = kp * inner
                row_ref[part, h : h + 1, :] = jnp.sum(joint, axis=0, keepdims=True)
                col_ref[part, :, h : h + 1] = jnp.sum(joint, axis=1, keepdims=True)
            mixed_ref[...] += mixed
            gx_ref[group, rows, lanes] = dot(jnp.concatenate(inners, axis=1), gm).astype(BF16)

        @pl.when(part == 1)
        def _():
            mixed_t = jnp.where(valid, mixed_ref[...], 0.0)
            db_ref[rows, lanes_n] = dot(mixed_t.astype(BF16), cc)
            dc_ref[rows, lanes_n] = dot(mixed_t.T.astype(BF16), bc)
            for at in range(2):
                diff_ref[group * chunks + c, at * few : (at + 1) * few, :] = row_ref[at] - col_ref[at].T[:few, :]

    def forward(k):
        return pltpu.make_async_remote_copy(
            src_ref=fs.at[k], dst_ref=ent_ref.at[k], send_sem=fsend.at[k], recv_sem=frecv.at[k],
            device_id=(pipe, right), device_id_type=MESH)

    def backward(k):
        return pltpu.make_async_remote_copy(
            src_ref=bs.at[k], dst_ref=adj_ref.at[k], send_sem=bsend.at[k], recv_sem=brecv.at[k],
            device_id=(pipe, left), device_id_type=MESH)

    def advance(k, place, make, got, local, sent):
        @pl.when(place > 0)
        def _():
            make(k).wait_recv()

        @pl.when(place == 0)
        def _():
            got[k] = jnp.zeros(got.shape[1:], BF16)

        @pl.when(place < n - 1)
        def _():
            sent[k] = (e_ref[k] * got[k].astype(F32) + local[k]).astype(BF16)
            make(k).start()

    def step(t, carry):
        kf = t - SKEW * me
        kb = t - SKEW * (n - 1 - me)

        @pl.when(jnp.logical_and(lax.rem(t, halves) == 0, t < PIECES))
        def _():
            states(lax.div(t, halves))

        @pl.when(t == 0)
        def _():
            pl.semaphore_wait(barrier, 2)

        @pl.when(jnp.logical_and(kf >= 0, kf < PIECES))
        def _():
            advance(kf, me, forward, ent_ref, s_ref, fs)

        @pl.when(jnp.logical_and(kb >= 0, kb < PIECES))
        def _():
            advance(kb, n - 1 - me, backward, adj_ref, a_ref, bs)

        @pl.when(t < 2 * G * chunks)
        def _():
            unit(lax.div(t, 2 * chunks), lax.rem(lax.div(t, 2), chunks), lax.rem(t, 2))

        return carry

    lax.fori_loop(0, max(SKEW * (n - 1) + PIECES, 2 * G * chunks), step, 0)

    first_adj_ref[...] = adj_ref[: RAW * halves]

    @pl.when(me < n - 1)
    def _():
        for k in range(PIECES):
            forward(k).wait_send()

    @pl.when(me > 0)
    def _():
        for k in range(PIECES):
            backward(k).wait_send()


def group_kernel(first, with_x, carried, x_ref, b_ref, c_ref, decay_ref, g_ref, skip_ref, ent_ref, adj_ref,
                 near_db_ref, near_dc_ref, diff_ref, *refs):
    refs = refs[carried:]
    if with_x:
        near_gx_ref, gx_ref, *refs = refs
        group = first + pl.program_id(0)
        own = iota((HPG, H), 1) == iota((HPG, H), 0) + group * HPG
        column = jnp.sum(jnp.where(own, skip_ref[...], 0.0), axis=1, keepdims=True)
    db_ref, dc_ref, gd_ref, es_ref, ds_ref = refs
    chunks = x_ref.shape[0] // Q
    square = (Q, Q)
    lower = ones_where(iota(square, 1) <= iota(square, 0))
    matrix = spread_matrix()
    heads = ones_where(iota((HPG, W), 0) == iota((HPG, W), 1) // P_SIZE)
    wide = heads.astype(F32)
    half = ent_ref.shape[2]
    if with_x:
        skip = jnp.sum(wide * column, axis=0, keepdims=True)

    for k in range(W // half):
        es_ref[0, :, k * half : (k + 1) * half] = ent_ref[k]
        ds_ref[chunks - 1, :, k * half : (k + 1) * half] = adj_ref[k]
    spans = [slice(c * Q, (c + 1) * Q) for c in range(chunks)]
    ends, xws, gws, keep = [], [], [], []
    for rows in spans:
        cum = columns_cumulative(decay_ref[:, rows] * LOG2E, lower)
        end = spread(jnp.exp2(cum[Q - 1 : Q, :] - cum), matrix)
        start = spread(jnp.exp2(cum), matrix)
        ends.append(end)
        xws.append((end * x_ref[rows, :].astype(F32)).astype(BF16))
        gws.append((start * g_ref[rows, :].astype(F32)).astype(BF16))
        keep.append(start[Q - 1 : Q, :])
    for c in range(chunks - 1):
        near = dot(b_ref[spans[c], :], xws[c], 0, 0)
        es_ref[c + 1] = (keep[c] * es_ref[c].astype(F32) + near).astype(BF16)
    for c in range(chunks - 1, 0, -1):
        near = dot(c_ref[spans[c], :], gws[c], 0, 0)
        ds_ref[c - 1] = (keep[c] * ds_ref[c].astype(F32) + near).astype(BF16)
    for c, rows in enumerate(spans):
        ent = es_ref[c]
        adj = ds_ref[c]
        edge = dot(b_ref[rows, :], adj)
        if with_x:
            gx_ref[rows, :] = (
                near_gx_ref[0, rows, :].astype(F32) + ends[c] * edge + skip * g_ref[rows, :].astype(F32)
            ).astype(BF16)
        db_ref[rows, :] = (near_db_ref[rows, :] + dot(xws[c], adj, 1, 1)).astype(BF16)
        dc_ref[rows, :] = (near_dc_ref[rows, :] + dot(gws[c], ent, 1, 1)).astype(BF16)
        right = xws[c].astype(F32) * edge
        left = gws[c].astype(F32) * dot(c_ref[rows, :], ent)
        both = left - right
        high = both.astype(BF16)
        low = (both - high.astype(F32)).astype(BF16)
        terms = dot(heads, high, 1, 1) + dot(heads, low, 1, 1)
        cross = keep[c] * jnp.sum(ent.astype(F32) * adj.astype(F32), axis=0, keepdims=True)
        rights = jnp.sum(right, axis=0, keepdims=True)
        last = jnp.sum(wide * (cross + rights), axis=1, keepdims=True)
        grads = diff_ref[c] + terms
        grads = grads + jnp.where(iota((HPG, Q), 1) == Q - 1, last, 0.0)
        gd_ref[:, rows] = sum(dot(part, lower) for part in split3(grads))


def place_kernel(piece_ref, whole_ref, out_ref):
    out_ref[...] = piece_ref[...]


def pack_kernel(heads, g_ref, b_ref, c_ref, decay_ref, skip_ref, raw_ref, out_ref):
    g_lanes, b_lanes = heads * P_SIZE, heads // HPG * N
    raw_ref[:, :g_lanes] = g_ref[...]
    raw_ref[:, g_lanes : g_lanes + b_lanes] = b_ref[...]
    raw_ref[:, g_lanes + b_lanes :] = c_ref[...]
    length = decay_ref.shape[1]
    out_ref[:, :length] = decay_ref[...]
    own = iota((heads, H), 0) == iota((heads, H), 1)
    column = jnp.sum(jnp.where(own, skip_ref[...], 0.0), axis=1, keepdims=True)
    out_ref[:, length:] = jnp.broadcast_to(column, (heads, 128))


def passed_kernel(g_ref, b_ref, c_ref, decay_ref, adj_ref, gx_ref, gw_ref, end_ref, ds_ref, edge_ref, cq_ref, cqt_ref):
    length = g_ref.shape[0]
    chunks = length // Q
    square = (Q, Q)
    lower = ones_where(iota(square, 1) <= iota(square, 0))
    upper = ones_where(iota(square, 0) <= iota(square, 1))
    matrix = spread_matrix()
    half = adj_ref.shape[2]
    for k in range(W // half):
        ds_ref[chunks - 1, :, k * half : (k + 1) * half] = adj_ref[k]
    wide = ones_where(iota((HPG, W), 0) == iota((HPG, W), 1) // P_SIZE).astype(F32)
    skip = jnp.sum(wide * decay_ref[:, length : length + 1], axis=0, keepdims=True)
    keep = []
    for c in range(chunks):
        rows = slice(c * Q, (c + 1) * Q)
        decay = decay_ref[:, rows] * LOG2E
        cum = columns_cumulative(decay, lower)
        cqt_ref[c] = cum
        cq_ref[c] = sum(dot(part, upper) for part in split3(decay))
        end_ref[rows, :] = spread(jnp.exp2(cum[Q - 1 : Q, :] - cum), matrix)
        start = spread(jnp.exp2(cum), matrix)
        gw_ref[rows, :] = (start * g_ref[rows, :].astype(F32)).astype(BF16)
        keep.append(start[Q - 1 : Q, :])
    for c in range(chunks - 1, 0, -1):
        rows = slice(c * Q, (c + 1) * Q)
        local = dot(c_ref[rows, :], gw_ref[rows, :], 0, 0)
        ds_ref[c - 1] = (keep[c] * ds_ref[c].astype(F32) + local).astype(BF16)

    def chunk(c, carry):
        rows = pl.ds(pl.multiple_of(c * Q, Q), Q)
        bc = b_ref[rows, :]
        valid = iota(square, 1) >= iota(square, 0)
        inner = jnp.where(valid, dot(bc, c_ref[rows, :], 1, 1), 0.0)
        edge_ref[...] = dot(bc, ds_ref[c])
        cqt = cqt_ref[c]
        low_lane = iota(square, 1) < P_SIZE
        for pair in range(HPG // 2):
            lanes = slice(pair * 128, (pair + 1) * 128)
            gp = g_ref[rows, lanes]
            zero = jnp.zeros_like(gp)
            gm = jnp.concatenate([jnp.where(low_lane, gp, zero), jnp.where(low_lane, zero, gp)], axis=0)
            inners = []
            for i in range(2):
                h = 2 * pair + i
                gap = jnp.minimum(cq_ref[c, h : h + 1, :] - cqt[:, h : h + 1], 0.0)
                inners.append((jnp.exp2(gap) * inner).astype(BF16))
            local = dot(jnp.concatenate(inners, axis=1), gm)
            gx_ref[rows, lanes] = (
                local + end_ref[rows, lanes] * edge_ref[:, lanes] + skip[:, lanes] * gp.astype(F32)
            ).astype(BF16)
        return carry

    lax.fori_loop(0, chunks, chunk, 0)


def local(ssm_input, input_proj, output_proj, log_decay, grad_output, skip_gain):
    x, b, c, decay, g = ssm_input[0], input_proj[0], output_proj[0], log_decay[0], grad_output[0]
    length = x.shape[0]
    chunks = length // Q
    n = lax.axis_size("ctx")
    half = G * W // PIECES
    halves = W // half
    devices = lax.axis_size("pipe")
    route = [(source, (source - 1) % devices) for source in range(devices)]

    def send(value):
        return lax.ppermute(value, "pipe", route)

    heads = RAW * HPG
    whole = pl.BlockSpec(memory_space=pltpu.VMEM)
    away = pl.BlockSpec(memory_space=pl.ANY)
    raw, raw_decay = pl.pallas_call(
        functools.partial(pack_kernel, heads),
        grid=(1,),
        in_specs=[
            pl.BlockSpec((length, RAW * W), lambda i: (0, 0)),
            pl.BlockSpec((length, RAW * N), lambda i: (0, 0)),
            pl.BlockSpec((length, RAW * N), lambda i: (0, 0)),
            pl.BlockSpec((heads, length), lambda i: (0, 0)),
            pl.BlockSpec((1, H), lambda i: (0, 0)),
        ],
        out_specs=[
            pl.BlockSpec((length, heads * P_SIZE + 2 * RAW * N), lambda i: (0, 0)),
            pl.BlockSpec((heads, length + 128), lambda i: (0, 0)),
        ],
        out_shape=[
            jax.ShapeDtypeStruct((length, heads * P_SIZE + 2 * RAW * N), BF16),
            jax.ShapeDtypeStruct((heads, length + 128), F32),
        ],
        compiler_params=pltpu.CompilerParams(vmem_limit_bytes=60 << 20),
        name="pack_raw",
    )(g, b, c, decay, skip_gain)
    raw = send(raw)
    raw_decay = send(raw_decay)

    states = jax.ShapeDtypeStruct((PIECES, N, half), BF16)
    entering, adjoint, near_gx, near_db, near_dc, diff, first_adjoint = pl.pallas_call(
        functools.partial(relay_kernel, n, halves, half),
        in_specs=[away] * 5,
        out_specs=[whole] * 7,
        out_shape=[
            states,
            states,
            jax.ShapeDtypeStruct((G, length, W), BF16),
            jax.ShapeDtypeStruct((length, G * N), F32),
            jax.ShapeDtypeStruct((length, G * N), F32),
            jax.ShapeDtypeStruct((G * chunks, HPG, Q), F32),
            jax.ShapeDtypeStruct((RAW * halves, N, half), BF16),
        ],
        scratch_shapes=[
            pltpu.VMEM((Q, Q), F32),
            pltpu.VMEM((2, HPG // 2, Q), F32),
            pltpu.VMEM((2, Q, Q), F32),
            pltpu.VMEM((G, length, W), BF16),
            pltpu.VMEM((length, G * N), BF16),
            pltpu.VMEM((length, G * N), BF16),
            pltpu.VMEM((H, length), F32),
            pltpu.VMEM((G, length, W), BF16),
            pltpu.VMEM((PIECES, N, half), F32),
            pltpu.VMEM((PIECES, N, half), F32),
            pltpu.VMEM((PIECES, 1, half), F32),
            pltpu.VMEM((PIECES, N, half), BF16),
            pltpu.VMEM((PIECES, N, half), BF16),
            pltpu.SemaphoreType.DMA((3,)),
            pltpu.SemaphoreType.DMA((2, G)),
        ] + [pltpu.SemaphoreType.DMA((PIECES,))] * 4,
        compiler_params=pltpu.CompilerParams(collective_id=0, has_side_effects=True, vmem_limit_bytes=60 << 20),
        cost_estimate=pl.CostEstimate(flops=30_000_000_000, bytes_accessed=8_000_000, transcendentals=1_000_000),
        name="relay",
    )(x, b, c, decay, g)
    raw_adjoint = send(first_adjoint)

    def own_groups(first, count, with_x, carry):
        pick = lambda i: (0, first + i)
        rows = lambda i: (first + i, 0)
        deep = lambda i: (first + i, 0, 0)
        pieces = pl.BlockSpec((halves, N, half), deep)
        out_specs = [
            pl.BlockSpec((length, W), lambda i: (0, i)),
            pl.BlockSpec((length, N), pick),
            pl.BlockSpec((length, N), pick),
            pl.BlockSpec((HPG, length), rows),
        ]
        out_shape = [
            jax.ShapeDtypeStruct((length, count * W), BF16),
            jax.ShapeDtypeStruct((length, G * N), BF16),
            jax.ShapeDtypeStruct((length, G * N), BF16),
            jax.ShapeDtypeStruct((H, length), F32),
        ]
        skipped = 0 if with_x else 1
        carried = len(carry)
        wide_in = [near_gx] if with_x else []
        return pl.pallas_call(
            functools.partial(group_kernel, first, with_x, carried),
            grid=(count,),
            in_specs=[
                pl.BlockSpec((length, W), pick),
                pl.BlockSpec((length, N), pick),
                pl.BlockSpec((length, N), pick),
                pl.BlockSpec((HPG, length), rows),
                pl.BlockSpec((length, W), pick),
                pl.BlockSpec((1, H), lambda i: (0, 0)),
                pieces,
                pieces,
                pl.BlockSpec((length, N), pick),
                pl.BlockSpec((length, N), pick),
                pl.BlockSpec((chunks, HPG, Q), deep),
            ] + [away] * carried + [pl.BlockSpec((1, length, W), deep)] * len(wide_in),
            out_specs=out_specs[skipped:],
            out_shape=out_shape[skipped:],
            input_output_aliases={11 + at: at + 1 - skipped for at in range(carried)},
            scratch_shapes=[pltpu.VMEM((chunks, N, W), BF16), pltpu.VMEM((chunks, N, W), BF16)],
            compiler_params=pltpu.CompilerParams(vmem_limit_bytes=60 << 20),
            cost_estimate=pl.CostEstimate(flops=3_000_000_000, bytes_accessed=4_000_000, transcendentals=1_000_000),
            name="group_grads",
        )(x, b, c, decay, g, skip_gain, entering, adjoint, near_db, near_dc, diff, *carry, *wide_in)

    sent = {}
    carry = ()
    for group in range(RAW, G):
        grads, *carry = own_groups(group, 1, True, carry)
        sent[group] = send(grads)
    grad_b, grad_c, grad_decay = own_groups(0, RAW, False, carry)
    grad_x = pl.pallas_call(
        passed_kernel,
        grid=(RAW,),
        in_specs=[
            pl.BlockSpec((length, W), lambda i: (0, i)),
            pl.BlockSpec((length, N), lambda i: (0, RAW * (W // N) + i)),
            pl.BlockSpec((length, N), lambda i: (0, RAW * (W // N) + RAW + i)),
            pl.BlockSpec((HPG, length + 128), lambda i: (i, 0)),
            pl.BlockSpec((halves, N, half), lambda i: (i, 0, 0)),
        ],
        out_specs=pl.BlockSpec((length, W), lambda i: (0, i)),
        out_shape=jax.ShapeDtypeStruct((length, G * W), BF16),
        scratch_shapes=[
            pltpu.VMEM((length, W), BF16),
            pltpu.VMEM((length, W), F32),
            pltpu.VMEM((chunks, N, W), BF16),
            pltpu.VMEM((Q, W), F32),
            pltpu.VMEM((chunks, HPG, Q), F32),
            pltpu.VMEM((chunks, Q, 2 * HPG), F32),
        ],
        compiler_params=pltpu.CompilerParams(vmem_limit_bytes=60 << 20),
        cost_estimate=pl.CostEstimate(flops=4_000_000_000, bytes_accessed=4_000_000, transcendentals=1_000_000),
        name="passed_grads",
    )(raw, raw, raw, raw_decay, raw_adjoint)
    for group in range(RAW, G):
        grad_x = pl.pallas_call(
            place_kernel,
            grid=(1,),
            in_specs=[pl.BlockSpec((length, W), lambda i: (0, 0)), away],
            out_specs=pl.BlockSpec((length, W), lambda i, group=group: (0, group)),
            out_shape=jax.ShapeDtypeStruct((length, G * W), BF16),
            input_output_aliases={1: 0},
            compiler_params=pltpu.CompilerParams(vmem_limit_bytes=60 << 20),
            name="place_grads",
        )(sent[group], grad_x)
    return grad_x[None], grad_b[None], grad_c[None], grad_decay[None]


def solution(mesh):
    return jax.shard_map(
        local,
        mesh=mesh,
        in_specs=(
            P("pipe", "ctx", None),
            P("pipe", "ctx", None),
            P("pipe", "ctx", None),
            P("pipe", None, "ctx"),
            P("pipe", "ctx", None),
            P("pipe", None),
        ),
        out_specs=(
            P("pipe", "ctx", None),
            P("pipe", "ctx", None),
            P("pipe", "ctx", None),
            P("pipe", None, "ctx"),
        ),
        check_vma=False,
    )
```

```python
import functools

import jax
import jax.numpy as jnp
from jax import lax
from jax.experimental import pallas as pl
from jax.experimental.pallas import tpu as pltpu
from jax.sharding import PartitionSpec as P

H = 64
P_SIZE = 64
N = 128
G = 4
HPG = 16
W = HPG * P_SIZE
Q = 128
PIECES = 8
SKEW = 2
RAW = 2
LOG2E = 1.4426950408889634
MESH = pl.DeviceIdType.MESH
F32 = jnp.float32
BF16 = jnp.bfloat16


def dot(a, b, ca=1, cb=0):
    return lax.dot_general(a, b, (((ca,), (cb,)), ((), ())), preferred_element_type=F32)


def iota(shape, axis):
    return lax.broadcasted_iota(jnp.int32, shape, axis)


def split3(value):
    high = value.astype(BF16)
    rest = value - high.astype(F32)
    middle = rest.astype(BF16)
    return high, middle, (rest - middle.astype(F32)).astype(BF16)


def ones_where(condition):
    return jnp.where(condition, 1.0, 0.0).astype(BF16)


def spread_matrix():
    shape = (2 * HPG, W)
    return ones_where(iota(shape, 0) % HPG == iota(shape, 1) // P_SIZE)


def spread(weights, matrix):
    high = weights.astype(BF16)
    low = (weights - high.astype(F32)).astype(BF16)
    first = iota(weights.shape, 1) < HPG
    return dot(jnp.where(first, high.astype(F32), low.astype(F32)).astype(BF16), matrix)


def columns_cumulative(decay, lower):
    twice = jnp.concatenate([decay, decay], axis=0)
    return sum(dot(lower, part, 1, 1) for part in split3(twice))


def relay_kernel(n, halves, half, x_hbm, b_hbm, c_hbm, decay_hbm, g_hbm, ent_ref, adj_ref, gx_ref, db_ref, dc_ref, diff_ref, first_adj_ref,
                 mixed_ref, row_ref, col_ref, xv, bv, cv, dv, gv, s_ref, a_ref, e_ref, fs, bs, small_sem, wide_sem, fsend, frecv, bsend, brecv):
    me = lax.axis_index("ctx")
    pipe = lax.axis_index("pipe")
    right, left = lax.rem(me + 1, n), lax.rem(me + n - 1, n)
    length = x_hbm.shape[0]
    small = [
        pltpu.make_async_copy(source, target, small_sem.at[at])
        for at, (source, target) in enumerate(((decay_hbm, dv), (b_hbm, bv), (c_hbm, cv)))
    ]

    def wide(group):
        lanes = pl.ds(pl.multiple_of(group * W, W), W)
        return (
            pltpu.make_async_copy(x_hbm.at[:, lanes], xv.at[group], wide_sem.at[0, group]),
            pltpu.make_async_copy(g_hbm.at[:, lanes], gv.at[group], wide_sem.at[1, group]),
        )

    for copy in small:
        copy.start()
    for group in range(G):
        for copy in wide(group):
            copy.start()
    barrier = pltpu.get_barrier_semaphore()
    for neighbour in (left, right):
        pl.semaphore_signal(barrier, inc=1, device_id=(pipe, neighbour), device_id_type=MESH)
    for copy in small:
        copy.wait()

    def states(group):
        for copy in wide(group):
            copy.wait()
        shape = (length, length)
        lower = ones_where(iota(shape, 1) <= iota(shape, 0))
        matrix = spread_matrix()
        decay = dv[pl.ds(pl.multiple_of(group * HPG, HPG), HPG), :]
        cum = columns_cumulative(decay * LOG2E, lower)
        lanes = pl.ds(pl.multiple_of(group * N, N), N)
        b = bv[:, lanes]
        c = cv[:, lanes]
        end = spread(jnp.exp2(cum[length - 1 : length, :] - cum), matrix)
        start = spread(jnp.exp2(cum), matrix)
        xw = (end * xv[group].astype(F32)).astype(BF16)
        gw = (start * gv[group].astype(F32)).astype(BF16)
        s = dot(b, xw, 0, 0)
        a = dot(c, gw, 0, 0)
        for k in range(halves):
            cut = slice(k * half, (k + 1) * half)
            s_ref[group * halves + k] = s[:, cut]
            a_ref[group * halves + k] = a[:, cut]
            e_ref[group * halves + k] = start[length - 1 : length, cut]

    chunks = length // Q
    col_ref[...] = jnp.zeros(col_ref.shape, F32)
    few = HPG // 2

    def unit(group, c, part):
        square = (Q, Q)
        lower = ones_where(iota(square, 1) <= iota(square, 0))
        upper = ones_where(iota(square, 0) <= iota(square, 1))
        rows = pl.ds(pl.multiple_of(c * Q, Q), Q)
        lanes_n = pl.ds(pl.multiple_of(group * N, N), N)
        pieces = split3(dv[pl.ds(pl.multiple_of(group * HPG + part * few, few), few), rows] * LOG2E)
        cqt = sum(dot(lower, piece, 1, 1) for piece in pieces)
        cq = sum(dot(piece, upper) for piece in pieces)
        bc = bv[rows, lanes_n]
        cc = cv[rows, lanes_n]
        valid = iota(square, 1) >= iota(square, 0)
        inner = jnp.where(valid, dot(bc, cc, 1, 1), 0.0)
        low_lane = iota(square, 1) < P_SIZE

        @pl.when(part == 0)
        def _():
            mixed_ref[...] = jnp.zeros(square, F32)

        for pair in range(few // 2):
            lanes = pl.ds(pl.multiple_of(part * (W // 2) + pair * 128, 128), 128)
            xp = xv[group, rows, lanes]
            gp = gv[group, rows, lanes]
            zero = jnp.zeros_like(gp)
            gm = jnp.concatenate([jnp.where(low_lane, gp, zero), jnp.where(low_lane, zero, gp)], axis=0)
            pair_prod = dot(xp, gm, 1, 1)
            inners = []
            mixed = None
            for i in range(2):
                h = 2 * pair + i
                kernel = jnp.exp2(jnp.minimum(cq[h : h + 1, :] - cqt[:, h : h + 1], 0.0))
                kp = kernel * pair_prod[:, i * Q : (i + 1) * Q]
                mixed = kp if mixed is None else mixed + kp
                inners.append((kernel * inner).astype(BF16))
                joint = kp * inner
                row_ref[part, h : h + 1, :] = jnp.sum(joint, axis=0, keepdims=True)
                col_ref[part, :, h : h + 1] = jnp.sum(joint, axis=1, keepdims=True)
            mixed_ref[...] += mixed
            gx_ref[group, rows, lanes] = dot(jnp.concatenate(inners, axis=1), gm).astype(BF16)

        @pl.when(part == 1)
        def _():
            mixed_t = jnp.where(valid, mixed_ref[...], 0.0)
            db_ref[rows, lanes_n] = dot(mixed_t.astype(BF16), cc)
            dc_ref[rows, lanes_n] = dot(mixed_t.T.astype(BF16), bc)
            for at in range(2):
                diff_ref[group * chunks + c, at * few : (at + 1) * few, :] = row_ref[at] - col_ref[at].T[:few, :]

    def forward(k):
        return pltpu.make_async_remote_copy(
            src_ref=fs.at[k], dst_ref=ent_ref.at[k], send_sem=fsend.at[k], recv_sem=frecv.at[k],
            device_id=(pipe, right), device_id_type=MESH)

    def backward(k):
        return pltpu.make_async_remote_copy(
            src_ref=bs.at[k], dst_ref=adj_ref.at[k], send_sem=bsend.at[k], recv_sem=brecv.at[k],
            device_id=(pipe, left), device_id_type=MESH)

    def advance(k, place, make, got, local, sent):
        @pl.when(place > 0)
        def _():
            make(k).wait_recv()

        @pl.when(place == 0)
        def _():
            got[k] = jnp.zeros(got.shape[1:], BF16)

        @pl.when(place < n - 1)
        def _():
            sent[k] = (e_ref[k] * got[k].astype(F32) + local[k]).astype(BF16)
            make(k).start()

    def step(t, carry):
        kf = t - SKEW * me
        kb = t - SKEW * (n - 1 - me)

        @pl.when(jnp.logical_and(lax.rem(t, halves) == 0, t < PIECES))
        def _():
            states(lax.div(t, halves))

        @pl.when(t == 0)
        def _():
            pl.semaphore_wait(barrier, 2)

        @pl.when(jnp.logical_and(kf >= 0, kf < PIECES))
        def _():
            advance(kf, me, forward, ent_ref, s_ref, fs)

        @pl.when(jnp.logical_and(kb >= 0, kb < PIECES))
        def _():
            advance(kb, n - 1 - me, backward, adj_ref, a_ref, bs)

        @pl.when(t < 2 * G * chunks)
        def _():
            unit(lax.div(t, 2 * chunks), lax.rem(lax.div(t, 2), chunks), lax.rem(t, 2))

        return carry

    lax.fori_loop(0, max(SKEW * (n - 1) + PIECES, 2 * G * chunks), step, 0)

    first_adj_ref[...] = adj_ref[: RAW * halves]

    @pl.when(me < n - 1)
    def _():
        for k in range(PIECES):
            forward(k).wait_send()

    @pl.when(me > 0)
    def _():
        for k in range(PIECES):
            backward(k).wait_send()


def group_kernel(first, with_x, carried, x_ref, b_ref, c_ref, decay_ref, g_ref, skip_ref, ent_ref, adj_ref,
                 near_db_ref, near_dc_ref, diff_ref, *refs):
    refs = refs[carried:]
    if with_x:
        near_gx_ref, gx_ref, *refs = refs
        group = first + pl.program_id(0)
        own = iota((HPG, H), 1) == iota((HPG, H), 0) + group * HPG
        column = jnp.sum(jnp.where(own, skip_ref[...], 0.0), axis=1, keepdims=True)
    db_ref, dc_ref, gd_ref, es_ref, ds_ref = refs
    chunks = x_ref.shape[0] // Q
    square = (Q, Q)
    lower = ones_where(iota(square, 1) <= iota(square, 0))
    matrix = spread_matrix()
    heads = ones_where(iota((HPG, W), 0) == iota((HPG, W), 1) // P_SIZE)
    wide = heads.astype(F32)
    half = ent_ref.shape[2]
    if with_x:
        skip = jnp.sum(wide * column, axis=0, keepdims=True)

    for k in range(W // half):
        es_ref[0, :, k * half : (k + 1) * half] = ent_ref[k]
        ds_ref[chunks - 1, :, k * half : (k + 1) * half] = adj_ref[k]
    spans = [slice(c * Q, (c + 1) * Q) for c in range(chunks)]
    ends, xws, gws, keep = [], [], [], []
    for rows in spans:
        cum = columns_cumulative(decay_ref[:, rows] * LOG2E, lower)
        end = spread(jnp.exp2(cum[Q - 1 : Q, :] - cum), matrix)
        start = spread(jnp.exp2(cum), matrix)
        ends.append(end)
        xws.append((end * x_ref[rows, :].astype(F32)).astype(BF16))
        gws.append((start * g_ref[rows, :].astype(F32)).astype(BF16))
        keep.append(start[Q - 1 : Q, :])
    for c in range(chunks - 1):
        near = dot(b_ref[spans[c], :], xws[c], 0, 0)
        es_ref[c + 1] = (keep[c] * es_ref[c].astype(F32) + near).astype(BF16)
    for c in range(chunks - 1, 0, -1):
        near = dot(c_ref[spans[c], :], gws[c], 0, 0)
        ds_ref[c - 1] = (keep[c] * ds_ref[c].astype(F32) + near).astype(BF16)
    for c, rows in enumerate(spans):
        ent = es_ref[c]
        adj = ds_ref[c]
        edge = dot(b_ref[rows, :], adj)
        if with_x:
            gx_ref[rows, :] = (
                near_gx_ref[0, rows, :].astype(F32) + ends[c] * edge + skip * g_ref[rows, :].astype(F32)
            ).astype(BF16)
        db_ref[rows, :] = (near_db_ref[rows, :] + dot(xws[c], adj, 1, 1)).astype(BF16)
        dc_ref[rows, :] = (near_dc_ref[rows, :] + dot(gws[c], ent, 1, 1)).astype(BF16)
        right = xws[c].astype(F32) * edge
        left = gws[c].astype(F32) * dot(c_ref[rows, :], ent)
        both = left - right
        high = both.astype(BF16)
        low = (both - high.astype(F32)).astype(BF16)
        terms = dot(heads, high, 1, 1) + dot(heads, low, 1, 1)
        cross = keep[c] * jnp.sum(ent.astype(F32) * adj.astype(F32), axis=0, keepdims=True)
        rights = jnp.sum(right, axis=0, keepdims=True)
        last = jnp.sum(wide * (cross + rights), axis=1, keepdims=True)
        grads = diff_ref[c] + terms
        grads = grads + jnp.where(iota((HPG, Q), 1) == Q - 1, last, 0.0)
        gd_ref[:, rows] = sum(dot(part, lower) for part in split3(grads))


def place_kernel(piece_ref, whole_ref, out_ref):
    out_ref[...] = piece_ref[...]


def pack_kernel(heads, g_ref, b_ref, c_ref, decay_ref, skip_ref, raw_ref):
    g_lanes, b_lanes = heads * P_SIZE, heads // HPG * N
    last = g_lanes + 2 * b_lanes
    raw_ref[:, :g_lanes] = g_ref[...]
    raw_ref[:, g_lanes : g_lanes + b_lanes] = b_ref[...]
    raw_ref[:, g_lanes + b_lanes : last] = c_ref[...]
    chunks = decay_ref.shape[1] // Q
    own = iota((heads, H), 0) == iota((heads, H), 1)
    column = jnp.sum(jnp.where(own, skip_ref[...], 0.0), axis=1, keepdims=True)
    blocks = [decay_ref[:, c * Q : (c + 1) * Q] for c in range(chunks)] + [jnp.broadcast_to(column, (heads, Q))]
    for at, block in enumerate(blocks):
        for part, piece in enumerate(split3(block)):
            row = (at * 3 + part) * heads
            raw_ref[row : row + heads, last:] = piece


def passed_kernel(heads, g_ref, b_ref, c_ref, scalars_ref, adj_ref, gx_ref, gw_ref, end_ref, ds_ref, edge_ref, cq_ref, cqt_ref):
    length = g_ref.shape[0]
    chunks = length // Q
    square = (Q, Q)
    lower = ones_where(iota(square, 1) <= iota(square, 0))
    upper = ones_where(iota(square, 0) <= iota(square, 1))
    matrix = spread_matrix()
    half = adj_ref.shape[2]
    for k in range(W // half):
        ds_ref[chunks - 1, :, k * half : (k + 1) * half] = adj_ref[k]
    wide = ones_where(iota((HPG, W), 0) == iota((HPG, W), 1) // P_SIZE).astype(F32)
    own = pl.program_id(0) * HPG

    def scalars(at):
        parts = [
            scalars_ref[pl.ds(pl.multiple_of((at * 3 + part) * heads + own, HPG), HPG), :].astype(F32) for part in range(3)
        ]
        return parts[0] + parts[1] + parts[2]

    skip = jnp.sum(wide * scalars(chunks)[:, :1], axis=0, keepdims=True)
    keep = []
    for c in range(chunks):
        rows = slice(c * Q, (c + 1) * Q)
        decay = scalars(c) * LOG2E
        cum = columns_cumulative(decay, lower)
        cqt_ref[c] = cum
        cq_ref[c] = sum(dot(part, upper) for part in split3(decay))
        end_ref[rows, :] = spread(jnp.exp2(cum[Q - 1 : Q, :] - cum), matrix)
        start = spread(jnp.exp2(cum), matrix)
        gw_ref[rows, :] = (start * g_ref[rows, :].astype(F32)).astype(BF16)
        keep.append(start[Q - 1 : Q, :])
    for c in range(chunks - 1, 0, -1):
        rows = slice(c * Q, (c + 1) * Q)
        local = dot(c_ref[rows, :], gw_ref[rows, :], 0, 0)
        ds_ref[c - 1] = (keep[c] * ds_ref[c].astype(F32) + local).astype(BF16)

    def chunk(c, carry):
        rows = pl.ds(pl.multiple_of(c * Q, Q), Q)
        bc = b_ref[rows, :]
        valid = iota(square, 1) >= iota(square, 0)
        inner = jnp.where(valid, dot(bc, c_ref[rows, :], 1, 1), 0.0)
        edge_ref[...] = dot(bc, ds_ref[c])
        cqt = cqt_ref[c]
        low_lane = iota(square, 1) < P_SIZE
        for pair in range(HPG // 2):
            lanes = slice(pair * 128, (pair + 1) * 128)
            gp = g_ref[rows, lanes]
            zero = jnp.zeros_like(gp)
            gm = jnp.concatenate([jnp.where(low_lane, gp, zero), jnp.where(low_lane, zero, gp)], axis=0)
            inners = []
            for i in range(2):
                h = 2 * pair + i
                gap = jnp.minimum(cq_ref[c, h : h + 1, :] - cqt[:, h : h + 1], 0.0)
                inners.append((jnp.exp2(gap) * inner).astype(BF16))
            local = dot(jnp.concatenate(inners, axis=1), gm)
            gx_ref[rows, lanes] = (
                local + end_ref[rows, lanes] * edge_ref[:, lanes] + skip[:, lanes] * gp.astype(F32)
            ).astype(BF16)
        return carry

    lax.fori_loop(0, chunks, chunk, 0)


def local(ssm_input, input_proj, output_proj, log_decay, grad_output, skip_gain):
    x, b, c, decay, g = ssm_input[0], input_proj[0], output_proj[0], log_decay[0], grad_output[0]
    length = x.shape[0]
    chunks = length // Q
    n = lax.axis_size("ctx")
    half = G * W // PIECES
    halves = W // half
    devices = lax.axis_size("pipe")
    route = [(source, (source - 1) % devices) for source in range(devices)]

    def send(value):
        return lax.ppermute(value, "pipe", route)

    heads = RAW * HPG
    whole = pl.BlockSpec(memory_space=pltpu.VMEM)
    away = pl.BlockSpec(memory_space=pl.ANY)
    raw_lanes = heads * P_SIZE + 2 * RAW * N + Q
    raw = pl.pallas_call(
        functools.partial(pack_kernel, heads),
        grid=(1,),
        in_specs=[
            pl.BlockSpec((length, RAW * W), lambda i: (0, 0)),
            pl.BlockSpec((length, RAW * N), lambda i: (0, 0)),
            pl.BlockSpec((length, RAW * N), lambda i: (0, 0)),
            pl.BlockSpec((heads, length), lambda i: (0, 0)),
            pl.BlockSpec((1, H), lambda i: (0, 0)),
        ],
        out_specs=pl.BlockSpec((length, raw_lanes), lambda i: (0, 0)),
        out_shape=jax.ShapeDtypeStruct((length, raw_lanes), BF16),
        compiler_params=pltpu.CompilerParams(vmem_limit_bytes=60 << 20),
        name="pack_raw",
    )(g, b, c, decay, skip_gain)
    raw = send(raw)

    states = jax.ShapeDtypeStruct((PIECES, N, half), BF16)
    entering, adjoint, near_gx, near_db, near_dc, diff, first_adjoint = pl.pallas_call(
        functools.partial(relay_kernel, n, halves, half),
        in_specs=[away] * 5,
        out_specs=[whole] * 7,
        out_shape=[
            states,
            states,
            jax.ShapeDtypeStruct((G, length, W), BF16),
            jax.ShapeDtypeStruct((length, G * N), F32),
            jax.ShapeDtypeStruct((length, G * N), F32),
            jax.ShapeDtypeStruct((G * chunks, HPG, Q), F32),
            jax.ShapeDtypeStruct((RAW * halves, N, half), BF16),
        ],
        scratch_shapes=[
            pltpu.VMEM((Q, Q), F32),
            pltpu.VMEM((2, HPG // 2, Q), F32),
            pltpu.VMEM((2, Q, Q), F32),
            pltpu.VMEM((G, length, W), BF16),
            pltpu.VMEM((length, G * N), BF16),
            pltpu.VMEM((length, G * N), BF16),
            pltpu.VMEM((H, length), F32),
            pltpu.VMEM((G, length, W), BF16),
            pltpu.VMEM((PIECES, N, half), F32),
            pltpu.VMEM((PIECES, N, half), F32),
            pltpu.VMEM((PIECES, 1, half), F32),
            pltpu.VMEM((PIECES, N, half), BF16),
            pltpu.VMEM((PIECES, N, half), BF16),
            pltpu.SemaphoreType.DMA((3,)),
            pltpu.SemaphoreType.DMA((2, G)),
        ] + [pltpu.SemaphoreType.DMA((PIECES,))] * 4,
        compiler_params=pltpu.CompilerParams(collective_id=0, has_side_effects=True, vmem_limit_bytes=60 << 20),
        cost_estimate=pl.CostEstimate(flops=30_000_000_000, bytes_accessed=8_000_000, transcendentals=1_000_000),
        name="relay",
    )(x, b, c, decay, g)
    raw_adjoint = send(first_adjoint)

    def own_groups(first, count, with_x, carry):
        pick = lambda i: (0, first + i)
        rows = lambda i: (first + i, 0)
        deep = lambda i: (first + i, 0, 0)
        pieces = pl.BlockSpec((halves, N, half), deep)
        out_specs = [
            pl.BlockSpec((length, W), lambda i: (0, i)),
            pl.BlockSpec((length, N), pick),
            pl.BlockSpec((length, N), pick),
            pl.BlockSpec((HPG, length), rows),
        ]
        out_shape = [
            jax.ShapeDtypeStruct((length, count * W), BF16),
            jax.ShapeDtypeStruct((length, G * N), BF16),
            jax.ShapeDtypeStruct((length, G * N), BF16),
            jax.ShapeDtypeStruct((H, length), F32),
        ]
        skipped = 0 if with_x else 1
        carried = len(carry)
        wide_in = [near_gx] if with_x else []
        return pl.pallas_call(
            functools.partial(group_kernel, first, with_x, carried),
            grid=(count,),
            in_specs=[
                pl.BlockSpec((length, W), pick),
                pl.BlockSpec((length, N), pick),
                pl.BlockSpec((length, N), pick),
                pl.BlockSpec((HPG, length), rows),
                pl.BlockSpec((length, W), pick),
                pl.BlockSpec((1, H), lambda i: (0, 0)),
                pieces,
                pieces,
                pl.BlockSpec((length, N), pick),
                pl.BlockSpec((length, N), pick),
                pl.BlockSpec((chunks, HPG, Q), deep),
            ] + [away] * carried + [pl.BlockSpec((1, length, W), deep)] * len(wide_in),
            out_specs=out_specs[skipped:],
            out_shape=out_shape[skipped:],
            input_output_aliases={11 + at: at + 1 - skipped for at in range(carried)},
            scratch_shapes=[pltpu.VMEM((chunks, N, W), BF16), pltpu.VMEM((chunks, N, W), BF16)],
            compiler_params=pltpu.CompilerParams(vmem_limit_bytes=60 << 20),
            cost_estimate=pl.CostEstimate(flops=300_000_000, bytes_accessed=400_000, transcendentals=1_000_000),
            name="group_grads",
        )(x, b, c, decay, g, skip_gain, entering, adjoint, near_db, near_dc, diff, *carry, *wide_in)

    sent = {}
    carry = ()
    for group in range(RAW, G):
        grads, *carry = own_groups(group, 1, True, carry)
        sent[group] = send(grads)
    grad_b, grad_c, grad_decay = own_groups(0, RAW, False, carry)
    grad_x = pl.pallas_call(
        functools.partial(passed_kernel, heads),
        grid=(RAW,),
        in_specs=[
            pl.BlockSpec((length, W), lambda i: (0, i)),
            pl.BlockSpec((length, N), lambda i: (0, RAW * (W // N) + i)),
            pl.BlockSpec((length, N), lambda i: (0, RAW * (W // N) + RAW + i)),
            pl.BlockSpec((length, Q), lambda i: (0, raw_lanes // Q - 1)),
            pl.BlockSpec((halves, N, half), lambda i: (i, 0, 0)),
        ],
        out_specs=pl.BlockSpec((length, W), lambda i: (0, i)),
        out_shape=jax.ShapeDtypeStruct((length, G * W), BF16),
        scratch_shapes=[
            pltpu.VMEM((length, W), BF16),
            pltpu.VMEM((length, W), F32),
            pltpu.VMEM((chunks, N, W), BF16),
            pltpu.VMEM((Q, W), F32),
            pltpu.VMEM((chunks, HPG, Q), F32),
            pltpu.VMEM((chunks, Q, 2 * HPG), F32),
        ],
        compiler_params=pltpu.CompilerParams(vmem_limit_bytes=24 << 20),
        cost_estimate=pl.CostEstimate(flops=4_000_000_000, bytes_accessed=400_000, transcendentals=1_000_000),
        name="passed_grads",
    )(raw, raw, raw, raw, raw_adjoint)
    for group in range(RAW, G):
        grad_x = pl.pallas_call(
            place_kernel,
            grid=(1,),
            in_specs=[pl.BlockSpec((length, W), lambda i: (0, 0)), away],
            out_specs=pl.BlockSpec((length, W), lambda i, group=group: (0, group)),
            out_shape=jax.ShapeDtypeStruct((length, G * W), BF16),
            input_output_aliases={1: 0},
            compiler_params=pltpu.CompilerParams(vmem_limit_bytes=8 << 20),
            name="place_grads",
        )(sent[group], grad_x)
    return grad_x[None], grad_b[None], grad_c[None], grad_decay[None]


def solution(mesh):
    return jax.shard_map(
        local,
        mesh=mesh,
        in_specs=(
            P("pipe", "ctx", None),
            P("pipe", "ctx", None),
            P("pipe", "ctx", None),
            P("pipe", None, "ctx"),
            P("pipe", "ctx", None),
            P("pipe", None),
        ),
        out_specs=(
            P("pipe", "ctx", None),
            P("pipe", "ctx", None),
            P("pipe", "ctx", None),
            P("pipe", None, "ctx"),
        ),
        check_vma=False,
    )
```
